512 devices in a mesh: chan: 64 (over y_hi, z, core), tm: 8 (over x, y_lo).
Axes of the slice: x: 4, y: 8 (y_hi: 4, y_lo: 2; y = y_hi * 2 + y_lo), z: 8, core: 2. Of those that a mesh axis runs over, the one named last changes fastest.
Arguments:
- strain: bfloat16 [8192, 4096], P('chan', 'tm'), may hold values from -6 to 6
- dead_counts: int32 [64], P('chan'), may hold values from 0 to 64
- partner: int32 [2, 64], replicated, may hold values from 0 to 63, as said below
Outputs:
- xcorr: float32 [128, 2097152], P(None, ('chan', 'tm'))
The draws below stay inside these ranges and needn't reach their ends.
Inputs may be any that keep to these rules, and one draw needn't show every extreme that they name: Each row r has a number s_r with 1 <= s_r < 64 and partner[r, i] = i XOR s_r (bitwise) for every block i; the s_r of different rows differ.
All inputs are finite; a program needn't handle non-finite values.
Results may differ from the reference program's by a relative error of at most 0.0066.
Values may be sent and summed in bfloat16 or wider, within the bound.
A program may use at most 64 MiB of HBM per device.

```python
import math
import jax
import jax.numpy as jnp
from jax import lax

NF = 2048
WH = 32
LAGS = 128
ROUNDS = 2
CB = 128
NT = 4096
BLOCKS = 64
CHANNELS = 8192


def draw_partner(key, part):
    order = jax.random.permutation(jax.random.fold_in(key, 17), BLOCKS - 1).astype(jnp.int32)
    masks = order[:ROUNDS] + 1
    block_ids = jnp.arange(BLOCKS, dtype=jnp.int32)
    table = jnp.bitwise_xor(block_ids[None, :], masks[:, None])
    return table.astype(jnp.int32)


def place_ends(entries, rng, low, high):
    longest = entries.shape.index(max(entries.shape))
    spots = []
    for shift in (0, 1):
        where = [jax.random.randint(jax.random.fold_in(rng, axis), (), 0, length) for axis, length in enumerate(entries.shape)]
        where[longest] = (where[longest] + shift) % entries.shape[longest]
        spots.append(tuple(where))
    return entries.at[spots[0]].set(low).at[spots[1]].set(high)


def level_of(key, dims, shards, least, largest):
    gain = 1.0
    for dim, parts in shards:
        steps = jax.random.uniform(jax.random.fold_in(jax.random.fold_in(key, 6), dim), (parts,), jnp.float32, least / len(shards), largest / len(shards))
        gain = gain * jnp.repeat(jnp.exp(steps), dims[dim] // parts).reshape((-1,) + (1,) * (len(dims) - 1 - dim))
    return gain


def bell_draw(own_key, extent, spread, limit, shards=(), kind=jnp.bfloat16):
    level = level_of(own_key, extent, shards, -0.22, 0.18) if shards else 1.0
    entries = jax.random.normal(own_key, extent, jnp.float32) * spread * level
    return jnp.minimum(jnp.maximum(entries, -limit), limit).astype(kind)


def setup_inputs(seed: int = 0) -> dict:
    keys = jax.random.split(jax.random.key(seed), 4)
    strain = bell_draw(keys[0], (CHANNELS, NT), 1.0, 6.0, ((0, 64), (1, 8)))
    dead_counts = place_ends(jax.random.randint(keys[1], (BLOCKS,), 0, CB // 2 + 1), jax.random.fold_in(keys[1], 1), 0, (CB // 2 + 1) - 1).astype(jnp.int32)
    partner = draw_partner(jax.random.fold_in(keys[3], 71), 0)
    return dict(strain=strain, dead_counts=dead_counts, partner=partner)


epsilon = 1e-05

def cross_spectra(mine, theirs):
    mine_re = mine[0].astype(jnp.float32).T
    mine_im = mine[1].astype(jnp.float32).T
    their_re = jnp.transpose(theirs[:, 0].astype(jnp.float32), (2, 1, 0))
    their_im = jnp.transpose(theirs[:, 1].astype(jnp.float32), (2, 1, 0))
    real_part = their_re[:, :, :, None] * mine_re[:, None, None, :] + their_im[:, :, :, None] * mine_im[:, None, None, :]
    imag_part = mine_im[:, None, None, :] * their_re[:, :, :, None] - mine_re[:, None, None, :] * their_im[:, :, :, None]
    bins = real_part.shape[0]
    real_part = real_part.reshape(bins, -1).astype(jnp.bfloat16)
    imag_part = imag_part.reshape(bins, -1).astype(jnp.bfloat16)
    return jnp.concatenate([real_part, imag_part], axis=0)

def inverse_table(freq_start, bins):
    freq_ids = freq_start + jnp.arange(bins, dtype=jnp.int32)
    lag_ids = jnp.arange(LAGS, dtype=jnp.int32)
    lags_mod = (lag_ids - LAGS // 2) % NT
    phase_index = lags_mod[:, None] * freq_ids[None, :] % NT
    phase = 2.0 * math.pi / NT * phase_index.astype(jnp.float32)
    amplitude = 2.0 / math.sqrt(NF)
    return jnp.concatenate([jnp.cos(phase) * amplitude, -jnp.sin(phase) * amplitude], axis=1).astype(jnp.bfloat16)

def reference(strain, dead_counts, partner):
    time_ids = jnp.arange(NT, dtype=jnp.int32)
    freq_ids = jnp.arange(NF, dtype=jnp.int32)
    phase_index = time_ids[:, None] * freq_ids[None, :] % NT
    phase = 2.0 * math.pi / NT * phase_index.astype(jnp.float32)
    amplitude = 1.0 / math.sqrt(NT)
    cos_table = (jnp.cos(phase) * amplitude).astype(jnp.bfloat16)
    sin_table = (-jnp.sin(phase) * amplitude).astype(jnp.bfloat16)
    spec_re = jnp.dot(strain, cos_table, preferred_element_type=jnp.float32)
    spec_im = jnp.dot(strain, sin_table, preferred_element_type=jnp.float32)
    spectral_power = spec_re * spec_re + spec_im * spec_im
    padded = jnp.pad(spectral_power, ((0, 0), (WH, WH)))
    total = jnp.zeros_like(spectral_power)
    for offset in range(2 * WH + 1):
        total = total + padded[:, offset:offset + NF]
    smooth = total * (1.0 / (2 * WH + 1))
    chan_ids = jnp.arange(CHANNELS, dtype=jnp.int32)
    alive_mask = (chan_ids % CB < CB - dead_counts[chan_ids // CB]).astype(jnp.float32)
    factor = alive_mask[:, None] * lax.rsqrt(smooth + epsilon)
    white_re = (spec_re * factor).astype(jnp.bfloat16)
    white_im = (spec_im * factor).astype(jnp.bfloat16)
    panels = jnp.stack([white_re, white_im], axis=0).reshape(2, BLOCKS, CB, NF)
    panels = jnp.transpose(panels, (1, 0, 2, 3))
    block_width = math.gcd(NF, 256)

    def one_block(block_id):
        mine = panels[block_id]
        theirs = jnp.take(panels, partner[:, block_id], axis=0)

        def add_block(turn, accum):
            start = (turn * block_width).astype(jnp.int32)
            mine_piece = lax.dynamic_slice_in_dim(mine, start, block_width, 2)
            their_piece = lax.dynamic_slice_in_dim(theirs, start, block_width, 3)
            spectra = cross_spectra(mine_piece, their_piece)
            table = inverse_table(start, block_width)
            return accum + jnp.dot(table, spectra, preferred_element_type=jnp.float32)
        empty = jnp.zeros((LAGS, CB * ROUNDS * CB), jnp.float32)
        return lax.fori_loop(0, NF // block_width, add_block, empty)
    results = lax.map(one_block, jnp.arange(BLOCKS, dtype=jnp.int32))
    return jnp.transpose(results, (1, 0, 2)).reshape(LAGS, BLOCKS * CB * ROUNDS * CB)
```

```python
import functools
import math

import jax
import jax.numpy as jnp
import numpy as np
from jax import lax
from jax.experimental import pallas as pl
from jax.experimental.pallas import tpu as pltpu
from jax.sharding import PartitionSpec as P

NF = 2048
WH = 32
LAGS = 128
NT = 4096
epsilon = 1e-05

R1 = 32
R2 = NF // R1
SEG = NT // R1
HALF = R1 // 2


def split_bf16(table):
    table = np.asarray(table, np.float32)
    high = table.astype(np.dtype(jnp.bfloat16)).astype(np.float32)
    return high, table - high


@functools.cache
def forward_constants():
    kappa, t1 = np.arange(R1), np.arange(R1)
    phase = 2 * np.pi * (kappa[:, None] * t1[None, :] % R1) / R1
    first = np.concatenate([np.cos(phase), -np.sin(phase)], axis=0)
    first = np.concatenate(split_bf16(first), axis=0)
    t0 = np.arange(SEG)
    phase = 2 * np.pi * (kappa[:, None] * t0[None, :]) / NT
    amplitude = 1 / math.sqrt(NT)
    twiddle = np.stack([np.cos(phase) * amplitude, np.sin(phase) * amplitude])
    k2 = np.arange(R2)
    phase = 2 * np.pi * (t0[:, None] * k2[None, :] % SEG) / SEG
    cos, sin = np.cos(phase), np.sin(phase)
    second = np.block([[cos, -sin], [sin, cos]])
    second = np.stack(split_bf16(second))
    return first.astype(np.float32), twiddle.astype(np.float32), second.astype(np.float32)


def window_sums(low, high):
    x = np.arange(-2 * NT, 2 * NT)
    u = np.arange(low, high)
    return np.exp(2j * np.pi * (x[:, None] * u[None, :] % NT) / NT).sum(1)


@functools.cache
def segment_table(low, high):
    sums = window_sums(low, high)
    f, k2 = np.arange(SEG), np.arange(R2)
    out = np.zeros((HALF, 2, 2, SEG, 2, 2, R2))
    for p in range(HALF):
        classes = (p, R1 - p) if p else (0, HALF)
        for h, target in enumerate(classes):
            for g, source in enumerate(classes):
                plus = np.zeros((SEG, R2), complex)
                minus = np.zeros((SEG, R2), complex)
                k = source + R1 * k2
                if source == target:
                    plus = sums[k[None, :] - R1 // 2 * f[:, None] - R1 // 4 + 2 * NT]
                if -source % R1 == target:
                    minus = sums[-k[None, :] - R1 // 2 * f[:, None] - R1 // 4 + 2 * NT]
                scale = np.ones(R2)
                if source == 0:
                    minus[:, 0] = 0
                    scale[0] = math.sqrt(2.0)
                real, imag = (plus + minus) * scale, 1j * (plus - minus) * scale
                out[p, h, 0, :, g, 0], out[p, h, 1, :, g, 0] = real.real, real.imag
                out[p, h, 0, :, g, 1], out[p, h, 1, :, g, 1] = imag.real, imag.imag
    return out.reshape(HALF, 4 * SEG, 4 * R2).astype(np.float32)


@functools.cache
def lag_table():
    tau, f = np.arange(LAGS) - LAGS // 2, np.arange(SEG)
    phase = 2 * np.pi * (f[None, :] + 0.5) * tau[:, None] / (2 * SEG)
    table = np.stack([np.cos(phase), -np.sin(phase)], axis=-1)
    scale = 1 / (2.0**19 * math.sqrt(2.0))
    return (table * scale).reshape(LAGS, 2 * SEG).astype(np.float32)


def greet(axis, count):
    me = lax.axis_index(axis)
    barrier = pltpu.get_barrier_semaphore()
    for step in range(1, count):
        peer = lax.rem(me + step, count)
        pl.semaphore_signal(
            barrier, inc=1, device_id={axis: peer}, device_id_type=pl.DeviceIdType.MESH
        )
    pl.semaphore_wait(barrier, count - 1)


def scatter_kernel(count, width, x_ref, o_ref, send_sem, recv_sem, own_sem):
    me = lax.axis_index("tm")
    greet("tm", count)
    copies = []
    for step in range(1, count):
        peer = lax.rem(me + step, count)
        copy = pltpu.make_async_remote_copy(
            src_ref=x_ref.at[pl.ds(pl.multiple_of(peer * width, width), width), :],
            dst_ref=o_ref.at[me],
            send_sem=send_sem.at[step],
            recv_sem=recv_sem.at[step],
            device_id={"tm": peer},
            device_id_type=pl.DeviceIdType.MESH,
        )
        copy.start()
        copies.append(copy)
    own = pltpu.make_async_copy(
        x_ref.at[pl.ds(pl.multiple_of(me * width, width), width), :], o_ref.at[me], own_sem
    )
    own.start()
    own.wait()
    for copy in copies:
        copy.wait()


def gather_kernel(count, x_ref, o_ref, send_sem, recv_sem, own_sem):
    me = lax.axis_index("tm")
    greet("tm", count)
    copies = []
    for step in range(1, count):
        peer = lax.rem(me + step, count)
        copy = pltpu.make_async_remote_copy(
            src_ref=x_ref,
            dst_ref=o_ref.at[me],
            send_sem=send_sem.at[step],
            recv_sem=recv_sem.at[step],
            device_id={"tm": peer},
            device_id_type=pl.DeviceIdType.MESH,
        )
        copy.start()
        copies.append(copy)
    own = pltpu.make_async_copy(x_ref, o_ref.at[me], own_sem)
    own.start()
    own.wait()
    for copy in copies:
        copy.wait()


def exchange(kernel, x, shape, count, collective_id):
    return pl.pallas_call(
        kernel,
        out_shape=jax.ShapeDtypeStruct(shape, x.dtype),
        in_specs=[pl.BlockSpec(memory_space=pl.ANY)],
        out_specs=pl.BlockSpec(memory_space=pl.ANY),
        scratch_shapes=[
            pltpu.SemaphoreType.DMA((count,)),
            pltpu.SemaphoreType.DMA((count,)),
            pltpu.SemaphoreType.DMA,
        ],
        compiler_params=pltpu.CompilerParams(collective_id=collective_id, has_side_effects=True),
    )(x)


def whiten_kernel(limit_ref, x_ref, first_ref, twiddle_ref, second_ref, o_ref, flat, spec):
    blocks, width, samples = x_ref.shape
    per = samples // SEG
    for j in range(blocks):
        for q in range(per):
            t1 = j * per + q
            flat[t1 * width : (t1 + 1) * width, :] = x_ref[
                j, :, q * SEG : (q + 1) * SEG
            ].astype(jnp.float32)
    cos, sin = twiddle_ref[0], twiddle_ref[1]
    for c in range(width):
        series = flat[pl.ds(c, R1, stride=width), :].astype(jnp.bfloat16)
        part = jnp.dot(first_ref[...], series, preferred_element_type=jnp.float32)
        real = part[:R1] + part[2 * R1 : 3 * R1]
        imag = part[R1 : 2 * R1] + part[3 * R1 :]
        turned = jnp.concatenate([real * cos + imag * sin, imag * cos - real * sin], axis=1)
        high = turned.astype(jnp.bfloat16)
        low = (turned - high.astype(jnp.float32)).astype(jnp.bfloat16)
        result = jnp.dot(high, second_ref[0], preferred_element_type=jnp.float32)
        result += jnp.dot(low, second_ref[0], preferred_element_type=jnp.float32)
        result += jnp.dot(high, second_ref[1], preferred_element_type=jnp.float32)
        spec[pl.ds(c, R1, stride=width), :] = result
    lane = lax.broadcasted_iota(jnp.int32, (width, 2 * R2), 1) % R2
    channel = lax.broadcasted_iota(jnp.int32, (width, 2 * R2), 0)
    alive = (channel < limit_ref[0]).astype(jnp.float32)
    power = []
    for kappa in range(R1):
        square = jnp.square(spec[kappa * width : (kappa + 1) * width, :])
        power.append(square + pltpu.roll(square, R2, 1))
    upto, total = [], None
    for kappa in range(R1):
        total = power[kappa] if total is None else total + power[kappa]
        upto.append(total)
    rest = None
    for kappa in reversed(range(R1)):
        rest = power[kappa] if rest is None else rest + power[kappa]
        below = jnp.where(lane == 0, 0.0, pltpu.roll(rest, 1, 1))
        above = jnp.where(lane == R2 - 1, 0.0, pltpu.roll(upto[kappa], 2 * R2 - 1, 1))
        smooth = (below + total + above) * (1.0 / (2 * WH + 1))
        factor = alive * lax.rsqrt(smooth + epsilon)
        piece = spec[kappa * width : (kappa + 1) * width, :] * factor
        o_ref[kappa] = piece.astype(jnp.bfloat16)


def whiten(limit, x):
    first, twiddle, second = forward_constants()
    _, width, _ = x.shape
    rows = R1 * width
    vmem = pl.BlockSpec(memory_space=pltpu.VMEM)
    return pl.pallas_call(
        whiten_kernel,
        out_shape=jax.ShapeDtypeStruct((R1, width, 2 * R2), jnp.bfloat16),
        in_specs=[pl.BlockSpec(memory_space=pltpu.SMEM)] + [vmem] * 4,
        out_specs=vmem,
        scratch_shapes=[
            pltpu.VMEM((rows, SEG), jnp.float32),
            pltpu.VMEM((rows, 2 * R2), jnp.float32),
        ],
    )(
        limit,
        x,
        jnp.asarray(first, jnp.bfloat16),
        jnp.asarray(twiddle, jnp.float32),
        jnp.asarray(second, jnp.bfloat16),
    )


def correlate_kernel(own_ref, *refs):
    rounds = len(refs) - 7
    their_refs = refs[:rounds]
    ta_ref, tb_ref, lag_ref, o_ref, aa, bb, ss = refs[rounds:]
    parts, _, width, lanes = own_ref.shape
    channels = parts * width
    pairs = rounds * width

    def transform(p, carry):
        one = p
        two = jnp.where(p == 0, HALF, R1 - p)
        mine = jnp.concatenate(
            [own_ref[:, k].reshape(channels, lanes) for k in (one, two)], axis=1
        )
        part = lax.dot_general(
            ta_ref[p], mine, (((1,), (1,)), ((), ())), preferred_element_type=jnp.float32
        )
        their = [jnp.concatenate([ref[k] for k in (one, two)], axis=1) for ref in their_refs]
        their = jnp.concatenate(their + their, axis=0)
        other = lax.dot_general(
            tb_ref[p], their, (((1,), (1,)), ((), ())), preferred_element_type=jnp.float32
        )
        left = lax.broadcasted_iota(jnp.int32, (SEG, 2 * pairs), 1) < pairs
        for h in range(2):
            for e in range(2):
                row = pl.ds(pl.multiple_of(((2 * h + e) * HALF + p) * SEG, SEG), SEG)
                start = (2 * h + e) * SEG
                aa[row, :] = part[start : start + SEG]
            real = other[2 * h * SEG : (2 * h + 1) * SEG]
            imag = other[(2 * h + 1) * SEG : (2 * h + 2) * SEG]
            row = pl.ds(pl.multiple_of((2 * h * HALF + p) * SEG, SEG), SEG)
            bb[row, : 2 * pairs] = jnp.where(left, real, -imag)
            row = pl.ds(pl.multiple_of(((2 * h + 1) * HALF + p) * SEG, SEG), SEG)
            bb[row, : 2 * pairs] = jnp.where(left, imag, real)
        return carry

    lax.fori_loop(0, HALF, transform, 0)

    def multiply(f, carry):
        mine = aa[pl.ds(f, 2 * R1, stride=SEG), :].astype(jnp.bfloat16)
        their = bb[pl.ds(f, 2 * R1, stride=SEG), :].astype(jnp.bfloat16)[:, : 2 * pairs]
        product = lax.dot_general(
            their, mine, (((0,), (0,)), ((), ())), preferred_element_type=jnp.float32
        )
        start = pl.multiple_of(f * 2 * pairs, 2 * pairs)
        ss[pl.ds(start, 2 * pairs), :] = product
        return carry

    lax.fori_loop(0, SEG, multiply, 0, unroll=4)

    for turn in range(rounds):
        for b in range(width):
            piece = ss[pl.ds(turn * width + b, 2 * SEG, stride=pairs), :].astype(jnp.bfloat16)
            start = (b * rounds + turn) * channels
            o_ref[:, start : start + channels] = jnp.dot(
                lag_ref[...], piece, preferred_element_type=jnp.float32
            )


def correlate(own, theirs):
    parts, _, width, lanes = own.shape
    channels = parts * width
    rounds = len(theirs)
    vmem = pl.BlockSpec(memory_space=pltpu.VMEM)
    return pl.pallas_call(
        correlate_kernel,
        out_shape=jax.ShapeDtypeStruct((LAGS, width * rounds * channels), jnp.float32),
        in_specs=[vmem] * (rounds + 4),
        out_specs=vmem,
        scratch_shapes=[
            pltpu.VMEM((4 * HALF * SEG, channels), jnp.float32),
            pltpu.VMEM((4 * HALF * SEG, 128), jnp.float32),
            pltpu.VMEM((SEG * 2 * rounds * width, channels), jnp.float32),
        ],
        compiler_params=pltpu.CompilerParams(vmem_limit_bytes=60 * 2**20),
    )(
        own,
        *theirs,
        jnp.asarray(segment_table(-LAGS // 2, SEG + LAGS // 2), jnp.bfloat16),
        jnp.asarray(segment_table(0, SEG), jnp.bfloat16),
        jnp.asarray(lag_table(), jnp.bfloat16),
    )


def partner_piece(piece, mask):
    count = lax.axis_size("chan")

    def route(bits):
        pairs = [(i, i ^ bits) for i in range(count)]
        return lambda held: lax.ppermute(held, "chan", pairs)

    return lax.switch(mask - 1, [route(bits) for bits in range(1, count)], piece)


def per_device(strain, dead_counts, partner):
    channels = strain.shape[0]
    tm_count = lax.axis_size("tm")
    width = channels // tm_count
    limit = channels - dead_counts - lax.axis_index("tm") * width
    samples = exchange(
        functools.partial(scatter_kernel, tm_count, width),
        strain,
        (tm_count, width, strain.shape[1]),
        tm_count,
        1,
    )
    piece = whiten(limit, samples)
    theirs = [partner_piece(piece, partner[turn, 0]) for turn in range(partner.shape[0])]
    own = exchange(
        functools.partial(gather_kernel, tm_count), piece, (tm_count,) + piece.shape, tm_count, 2
    )
    return correlate(own, theirs)


def solution(mesh):
    return jax.shard_map(
        per_device,
        mesh=mesh,
        in_specs=(P("chan", "tm"), P("chan"), P()),
        out_specs=P(None, ("chan", "tm")),
        check_vma=False,
    )
```

```python
import functools
import math

import jax
import jax.numpy as jnp
import numpy as np
from jax import lax
from jax.experimental import pallas as pl
from jax.experimental.pallas import tpu as pltpu
from jax.sharding import PartitionSpec as P

NF = 2048
WH = 32
LAGS = 128
NT = 4096
epsilon = 1e-05

R1 = 32
R2 = NF // R1
SEG = NT // R1
HALF = R1 // 2


def split_bf16(table):
    table = np.asarray(table, np.float32)
    high = table.astype(np.dtype(jnp.bfloat16)).astype(np.float32)
    return high, table - high


@functools.cache
def forward_constants():
    kappa, t1 = np.arange(R1), np.arange(R1)
    phase = 2 * np.pi * (kappa[:, None] * t1[None, :] % R1) / R1
    first = np.concatenate([np.cos(phase), -np.sin(phase)], axis=0)
    first = np.concatenate(split_bf16(first), axis=0)
    t0 = np.arange(SEG)
    phase = 2 * np.pi * (kappa[:, None] * t0[None, :]) / NT
    amplitude = 1 / math.sqrt(NT)
    twiddle = np.stack([np.cos(phase) * amplitude, np.sin(phase) * amplitude])
    k2 = np.arange(R2)
    phase = 2 * np.pi * (t0[:, None] * k2[None, :] % SEG) / SEG
    cos, sin = np.cos(phase), np.sin(phase)
    second = np.block([[cos, -sin], [sin, cos]])
    second = np.stack(split_bf16(second))
    return first.astype(np.float32), twiddle.astype(np.float32), second.astype(np.float32)


def window_sums(low, high):
    x = np.arange(-2 * NT, 2 * NT)
    u = np.arange(low, high)
    return np.exp(2j * np.pi * (x[:, None] * u[None, :] % NT) / NT).sum(1)


@functools.cache
def segment_table(low, high):
    sums = window_sums(low, high)
    f, k2 = np.arange(SEG), np.arange(R2)
    out = np.zeros((HALF, 2, 2, SEG, 2, 2, R2))
    for p in range(HALF):
        classes = (p, R1 - p) if p else (0, HALF)
        for h, target in enumerate(classes):
            for g, source in enumerate(classes):
                plus = np.zeros((SEG, R2), complex)
                minus = np.zeros((SEG, R2), complex)
                k = source + R1 * k2
                if source == target:
                    plus = sums[k[None, :] - R1 // 2 * f[:, None] - R1 // 4 + 2 * NT]
                if -source % R1 == target:
                    minus = sums[-k[None, :] - R1 // 2 * f[:, None] - R1 // 4 + 2 * NT]
                scale = np.ones(R2)
                if source == 0:
                    minus[:, 0] = 0
                    scale[0] = math.sqrt(2.0)
                real, imag = (plus + minus) * scale, 1j * (plus - minus) * scale
                out[p, h, 0, :, g, 0], out[p, h, 1, :, g, 0] = real.real, real.imag
                out[p, h, 0, :, g, 1], out[p, h, 1, :, g, 1] = imag.real, imag.imag
    return out.reshape(HALF, 4 * SEG, 4 * R2).astype(np.float32)


@functools.cache
def lag_table():
    tau, f = np.arange(LAGS) - LAGS // 2, np.arange(SEG)
    phase = 2 * np.pi * (f[None, :] + 0.5) * tau[:, None] / (2 * SEG)
    table = np.stack([np.cos(phase), -np.sin(phase)], axis=-1)
    scale = 1 / (2.0**19 * math.sqrt(2.0))
    return (table * scale).reshape(LAGS, 2 * SEG).astype(np.float32)


def greet(axis, count):
    me = lax.axis_index(axis)
    barrier = pltpu.get_barrier_semaphore()
    for step in range(1, count):
        peer = lax.rem(me + step, count)
        pl.semaphore_signal(
            barrier, inc=1, device_id={axis: peer}, device_id_type=pl.DeviceIdType.MESH
        )
    pl.semaphore_wait(barrier, count - 1)


def scatter_kernel(count, width, x_ref, o_ref, send_sem, recv_sem, own_sem):
    me = lax.axis_index("tm")
    greet("tm", count)
    copies = []
    for step in range(1, count):
        peer = lax.rem(me + step, count)
        copy = pltpu.make_async_remote_copy(
            src_ref=x_ref.at[pl.ds(pl.multiple_of(peer * width, width), width), :],
            dst_ref=o_ref.at[me],
            send_sem=send_sem.at[step],
            recv_sem=recv_sem.at[step],
            device_id={"tm": peer},
            device_id_type=pl.DeviceIdType.MESH,
        )
        copy.start()
        copies.append(copy)
    own = pltpu.make_async_copy(
        x_ref.at[pl.ds(pl.multiple_of(me * width, width), width), :], o_ref.at[me], own_sem
    )
    own.start()
    own.wait()
    for copy in copies:
        copy.wait()


def gather_kernel(count, x_ref, o_ref, send_sem, recv_sem, own_sem):
    me = lax.axis_index("tm")
    greet("tm", count)
    copies = []
    for step in range(1, count):
        peer = lax.rem(me + step, count)
        copy = pltpu.make_async_remote_copy(
            src_ref=x_ref,
            dst_ref=o_ref.at[me],
            send_sem=send_sem.at[step],
            recv_sem=recv_sem.at[step],
            device_id={"tm": peer},
            device_id_type=pl.DeviceIdType.MESH,
        )
        copy.start()
        copies.append(copy)
    own = pltpu.make_async_copy(x_ref, o_ref.at[me], own_sem)
    own.start()
    own.wait()
    for copy in copies:
        copy.wait()


def exchange(kernel, x, shape, count, collective_id):
    return pl.pallas_call(
        kernel,
        out_shape=jax.ShapeDtypeStruct(shape, x.dtype),
        in_specs=[pl.BlockSpec(memory_space=pl.ANY)],
        out_specs=pl.BlockSpec(memory_space=pl.ANY),
        scratch_shapes=[
            pltpu.SemaphoreType.DMA((count,)),
            pltpu.SemaphoreType.DMA((count,)),
            pltpu.SemaphoreType.DMA,
        ],
        compiler_params=pltpu.CompilerParams(
            collective_id=collective_id, has_side_effects=True, skip_device_barrier=True
        ),
    )(x)


def whiten_kernel(limit_ref, x_ref, first_ref, twiddle_ref, second_ref, o_ref, flat, spec):
    blocks, width, samples = x_ref.shape
    per = samples // SEG
    for j in range(blocks):
        for q in range(per):
            t1 = j * per + q
            flat[t1 * width : (t1 + 1) * width, :] = x_ref[
                j, :, q * SEG : (q + 1) * SEG
            ].astype(jnp.float32)
    cos, sin = twiddle_ref[0], twiddle_ref[1]
    for c in range(width):
        series = flat[pl.ds(c, R1, stride=width), :].astype(jnp.bfloat16)
        part = jnp.dot(first_ref[...], series, preferred_element_type=jnp.float32)
        real = part[:R1] + part[2 * R1 : 3 * R1]
        imag = part[R1 : 2 * R1] + part[3 * R1 :]
        turned = jnp.concatenate([real * cos + imag * sin, imag * cos - real * sin], axis=1)
        high = turned.astype(jnp.bfloat16)
        low = (turned - high.astype(jnp.float32)).astype(jnp.bfloat16)
        result = jnp.dot(high, second_ref[0], preferred_element_type=jnp.float32)
        result += jnp.dot(low, second_ref[0], preferred_element_type=jnp.float32)
        result += jnp.dot(high, second_ref[1], preferred_element_type=jnp.float32)
        spec[pl.ds(c, R1, stride=width), :] = result
    lane = lax.broadcasted_iota(jnp.int32, (width, 2 * R2), 1) % R2
    channel = lax.broadcasted_iota(jnp.int32, (width, 2 * R2), 0)
    alive = (channel < limit_ref[0]).astype(jnp.float32)
    power = []
    for kappa in range(R1):
        square = jnp.square(spec[kappa * width : (kappa + 1) * width, :])
        power.append(square + pltpu.roll(square, R2, 1))
    upto, total = [], None
    for kappa in range(R1):
        total = power[kappa] if total is None else total + power[kappa]
        upto.append(total)
    rest = None
    for kappa in reversed(range(R1)):
        rest = power[kappa] if rest is None else rest + power[kappa]
        below = jnp.where(lane == 0, 0.0, pltpu.roll(rest, 1, 1))
        above = jnp.where(lane == R2 - 1, 0.0, pltpu.roll(upto[kappa], 2 * R2 - 1, 1))
        smooth = (below + total + above) * (1.0 / (2 * WH + 1))
        factor = alive * lax.rsqrt(smooth + epsilon)
        piece = spec[kappa * width : (kappa + 1) * width, :] * factor
        o_ref[kappa] = piece.astype(jnp.bfloat16)


def whiten(limit, x):
    first, twiddle, second = forward_constants()
    _, width, _ = x.shape
    rows = R1 * width
    vmem = pl.BlockSpec(memory_space=pltpu.VMEM)
    return pl.pallas_call(
        whiten_kernel,
        out_shape=jax.ShapeDtypeStruct((R1, width, 2 * R2), jnp.bfloat16),
        in_specs=[pl.BlockSpec(memory_space=pltpu.SMEM)] + [vmem] * 4,
        out_specs=vmem,
        scratch_shapes=[
            pltpu.VMEM((rows, SEG), jnp.float32),
            pltpu.VMEM((rows, 2 * R2), jnp.float32),
        ],
    )(
        limit,
        x,
        jnp.asarray(first, jnp.bfloat16),
        jnp.asarray(twiddle, jnp.float32),
        jnp.asarray(second, jnp.bfloat16),
    )


def correlate_kernel(own_ref, *refs):
    rounds = len(refs) - 7
    their_refs = refs[:rounds]
    ta_ref, tb_ref, lag_ref, o_ref, aa, bb, ss = refs[rounds:]
    parts, _, width, lanes = own_ref.shape
    channels = parts * width
    pairs = rounds * width

    def transform(p, carry):
        one = p
        two = jnp.where(p == 0, HALF, R1 - p)
        mine = jnp.concatenate(
            [own_ref[:, k].reshape(channels, lanes) for k in (one, two)], axis=1
        )
        part = lax.dot_general(
            ta_ref[p], mine, (((1,), (1,)), ((), ())), preferred_element_type=jnp.float32
        )
        their = [jnp.concatenate([ref[k] for k in (one, two)], axis=1) for ref in their_refs]
        their = jnp.concatenate(their + their, axis=0)
        other = lax.dot_general(
            tb_ref[p], their, (((1,), (1,)), ((), ())), preferred_element_type=jnp.float32
        )
        left = lax.broadcasted_iota(jnp.int32, (SEG, 2 * pairs), 1) < pairs
        for h in range(2):
            for e in range(2):
                row = pl.ds(pl.multiple_of(((2 * h + e) * HALF + p) * SEG, SEG), SEG)
                start = (2 * h + e) * SEG
                aa[row, :] = part[start : start + SEG]
            real = other[2 * h * SEG : (2 * h + 1) * SEG]
            imag = other[(2 * h + 1) * SEG : (2 * h + 2) * SEG]
            row = pl.ds(pl.multiple_of((2 * h * HALF + p) * SEG, SEG), SEG)
            bb[row, : 2 * pairs] = jnp.where(left, real, -imag)
            row = pl.ds(pl.multiple_of(((2 * h + 1) * HALF + p) * SEG, SEG), SEG)
            bb[row, : 2 * pairs] = jnp.where(left, imag, real)
        return carry

    lax.fori_loop(0, HALF, transform, 0)

    def multiply(f, carry):
        mine = aa[pl.ds(f, 2 * R1, stride=SEG), :].astype(jnp.bfloat16)
        their = bb[pl.ds(f, 2 * R1, stride=SEG), :].astype(jnp.bfloat16)[:, : 2 * pairs]
        product = lax.dot_general(
            their, mine, (((0,), (0,)), ((), ())), preferred_element_type=jnp.float32
        )
        start = pl.multiple_of(f * 2 * pairs, 2 * pairs)
        ss[pl.ds(start, 2 * pairs), :] = product
        return carry

    lax.fori_loop(0, SEG, multiply, 0, unroll=4)

    for turn in range(rounds):
        for b in range(width):
            piece = ss[pl.ds(turn * width + b, 2 * SEG, stride=pairs), :].astype(jnp.bfloat16)
            start = (b * rounds + turn) * channels
            o_ref[:, start : start + channels] = jnp.dot(
                lag_ref[...], piece, preferred_element_type=jnp.float32
            )


def correlate(own, theirs):
    parts, _, width, lanes = own.shape
    channels = parts * width
    rounds = len(theirs)
    vmem = pl.BlockSpec(memory_space=pltpu.VMEM)
    return pl.pallas_call(
        correlate_kernel,
        out_shape=jax.ShapeDtypeStruct((LAGS, width * rounds * channels), jnp.float32),
        in_specs=[vmem] * (rounds + 4),
        out_specs=vmem,
        scratch_shapes=[
            pltpu.VMEM((4 * HALF * SEG, channels), jnp.float32),
            pltpu.VMEM((4 * HALF * SEG, 128), jnp.float32),
            pltpu.VMEM((SEG * 2 * rounds * width, channels), jnp.float32),
        ],
        compiler_params=pltpu.CompilerParams(vmem_limit_bytes=60 * 2**20),
    )(
        own,
        *theirs,
        jnp.asarray(segment_table(-LAGS // 2, SEG + LAGS // 2), jnp.bfloat16),
        jnp.asarray(segment_table(0, SEG), jnp.bfloat16),
        jnp.asarray(lag_table(), jnp.bfloat16),
    )


def permuted(bits, count):
    pairs = [(i, i ^ bits) for i in range(count)]
    return lambda held: lax.ppermute(held, "chan", pairs)


def partner_piece(piece, beside, mask):
    count = lax.axis_size("chan")
    held = jnp.where(mask % 2 == 1, beside, piece)
    routes = [lambda held: held] + [permuted(bits, count) for bits in range(2, count, 2)]
    return lax.switch(mask // 2, routes, held)


def per_device(strain, dead_counts, partner):
    channels = strain.shape[0]
    tm_count = lax.axis_size("tm")
    width = channels // tm_count
    limit = channels - dead_counts - lax.axis_index("tm") * width
    samples = exchange(
        functools.partial(scatter_kernel, tm_count, width),
        strain,
        (tm_count, width, strain.shape[1]),
        tm_count,
        1,
    )
    piece = whiten(limit, samples)
    beside = permuted(1, lax.axis_size("chan"))(piece)
    theirs = [partner_piece(piece, beside, partner[turn, 0]) for turn in range(partner.shape[0])]
    own = exchange(
        functools.partial(gather_kernel, tm_count), piece, (tm_count,) + piece.shape, tm_count, 2
    )
    return correlate(own, theirs)


def solution(mesh):
    return jax.shard_map(
        per_device,
        mesh=mesh,
        in_specs=(P("chan", "tm"), P("chan"), P()),
        out_specs=P(None, ("chan", "tm")),
        check_vma=False,
    )
```

```python
import functools
import math

import jax
import jax.numpy as jnp
import numpy as np
from jax import lax
from jax.experimental import pallas as pl
from jax.experimental.pallas import tpu as pltpu
from jax.sharding import PartitionSpec as P

NF = 2048
WH = 32
LAGS = 128
NT = 4096
epsilon = 1e-05

R1 = 32
R2 = NF // R1
SEG = NT // R1
HALF = R1 // 2


def split_bf16(table):
    table = np.asarray(table, np.float32)
    high = table.astype(np.dtype(jnp.bfloat16)).astype(np.float32)
    return high, table - high


@functools.cache
def forward_constants():
    kappa, t1 = np.arange(R1), np.arange(R1)
    phase = 2 * np.pi * (kappa[:, None] * t1[None, :] % R1) / R1
    first = np.concatenate([np.cos(phase), -np.sin(phase)], axis=0)
    first = np.concatenate(split_bf16(first), axis=0)
    t0 = np.arange(SEG)
    phase = 2 * np.pi * (kappa[:, None] * t0[None, :]) / NT
    amplitude = 1 / math.sqrt(NT)
    twiddle = np.stack([np.cos(phase) * amplitude, np.sin(phase) * amplitude])
    k2 = np.arange(R2)
    phase = 2 * np.pi * (t0[:, None] * k2[None, :] % SEG) / SEG
    cos, sin = np.cos(phase), np.sin(phase)
    second = np.block([[cos, -sin], [sin, cos]])
    second = np.stack(split_bf16(second))
    return first.astype(np.float32), twiddle.astype(np.float32), second.astype(np.float32)


def window_sums(low, high):
    x = np.arange(-2 * NT, 2 * NT)
    u = np.arange(low, high)
    return np.exp(2j * np.pi * (x[:, None] * u[None, :] % NT) / NT).sum(1)


@functools.cache
def segment_table(low, high):
    sums = window_sums(low, high)
    f, k2 = np.arange(SEG), np.arange(R2)
    out = np.zeros((HALF, 2, 2, SEG, 2, 2, R2))
    for p in range(HALF):
        classes = (p, R1 - p) if p else (0, HALF)
        for h, target in enumerate(classes):
            for g, source in enumerate(classes):
                plus = np.zeros((SEG, R2), complex)
                minus = np.zeros((SEG, R2), complex)
                k = source + R1 * k2
                if source == target:
                    plus = sums[k[None, :] - R1 // 2 * f[:, None] - R1 // 4 + 2 * NT]
                if -source % R1 == target:
                    minus = sums[-k[None, :] - R1 // 2 * f[:, None] - R1 // 4 + 2 * NT]
                scale = np.ones(R2)
                if source == 0:
                    minus[:, 0] = 0
                    scale[0] = math.sqrt(2.0)
                real, imag = (plus + minus) * scale, 1j * (plus - minus) * scale
                out[p, h, 0, :, g, 0], out[p, h, 1, :, g, 0] = real.real, real.imag
                out[p, h, 0, :, g, 1], out[p, h, 1, :, g, 1] = imag.real, imag.imag
    return out.reshape(HALF, 4 * SEG, 4 * R2).astype(np.float32)


@functools.cache
def lag_table():
    tau, f = np.arange(LAGS) - LAGS // 2, np.arange(SEG)
    phase = 2 * np.pi * (f[None, :] + 0.5) * tau[:, None] / (2 * SEG)
    table = np.stack([np.cos(phase), -np.sin(phase)], axis=-1)
    scale = 1 / (2.0**19 * math.sqrt(2.0))
    return (table * scale).reshape(LAGS, 2 * SEG).astype(np.float32)


MESH = pl.DeviceIdType.MESH


def signal(**target):
    barrier = pltpu.get_barrier_semaphore()
    pl.semaphore_signal(barrier, inc=1, device_id=target, device_id_type=MESH)


def send(src, dst, sems, index, **target):
    copy = pltpu.make_async_remote_copy(
        src_ref=src,
        dst_ref=dst,
        send_sem=sems[0].at[index],
        recv_sem=sems[1].at[index],
        device_id=target,
        device_id_type=MESH,
    )
    copy.start()
    return copy


def scatter_kernel(count, width, x_ref, o_ref, send_sem, recv_sem, own_sem):
    me = lax.axis_index("tm")
    peers = [lax.rem(me + step, count) for step in range(1, count)]
    for peer in peers:
        signal(tm=peer)
    pl.semaphore_wait(pltpu.get_barrier_semaphore(), len(peers))

    def rows(index):
        return x_ref.at[pl.ds(pl.multiple_of(index * width, width), width), :]

    copies = [
        send(rows(peer), o_ref.at[me], (send_sem, recv_sem), step, tm=peer)
        for step, peer in enumerate(peers)
    ]
    own = pltpu.make_async_copy(rows(me), o_ref.at[me], own_sem)
    own.start()
    own.wait()
    for copy in copies:
        copy.wait()


def scatter(strain, count, width):
    return pl.pallas_call(
        functools.partial(scatter_kernel, count, width),
        out_shape=jax.ShapeDtypeStruct((count, width, strain.shape[1]), strain.dtype),
        in_specs=[pl.BlockSpec(memory_space=pltpu.VMEM)],
        out_specs=pl.BlockSpec(memory_space=pl.ANY),
        scratch_shapes=[
            pltpu.SemaphoreType.DMA((count,)),
            pltpu.SemaphoreType.DMA((count,)),
            pltpu.SemaphoreType.DMA,
        ],
        compiler_params=pltpu.CompilerParams(
            collective_id=32, has_side_effects=True, skip_device_barrier=True
        ),
    )(strain)


def swap_kernel(bits, count, low_ref, high_ref, mine_ref, their_ref, all_ref, *sems):
    pair_sems, over_sems, gather_sems, own_sem = sems[0:2], sems[2:4], sems[4:6], sems[6]
    me, block = lax.axis_index("tm"), lax.axis_index("chan")
    peers = [lax.rem(me + step, count) for step in range(1, count)]
    partner = block
    for digit in range(bits.bit_length()):
        if bits >> digit & 1:
            partner = partner + 2**digit * (1 - 2 * (block // 2**digit % 2))
    beside = block + 1 - 2 * (block % 2)
    signal(chan=beside)
    if bits:
        signal(chan=partner)
    for peer in peers:
        signal(tm=peer)
    pl.semaphore_wait(pltpu.get_barrier_semaphore(), len(peers) + 1 + (bits > 0))
    halves = (low_ref, high_ref)
    if bits:
        pair = [
            send(half, their_ref.at[0, h], pair_sems, h, chan=partner)
            for h, half in enumerate(halves)
        ]
    else:
        pair = [
            pltpu.make_async_copy(half, their_ref.at[0, h], pair_sems[0].at[h])
            for h, half in enumerate(halves)
        ]
        for copy in pair:
            copy.start()
    copies = [
        send(mine_ref, all_ref.at[me], gather_sems, step, tm=peer)
        for step, peer in enumerate(peers)
    ]
    own = pltpu.make_async_copy(mine_ref, all_ref.at[me], own_sem)
    own.start()
    for h, copy in enumerate(pair):
        if bits:
            copy.wait_recv()
        else:
            copy.wait()
        copies.append(send(their_ref.at[0, h], their_ref.at[1, h], over_sems, h, chan=beside))
    if bits:
        for copy in pair:
            copy.wait_send()
    own.wait()
    for copy in copies:
        copy.wait()


def swap(bits, count, low, high, mine):
    here = pl.BlockSpec(memory_space=pltpu.VMEM)
    there = pl.BlockSpec(memory_space=pl.ANY)
    return pl.pallas_call(
        functools.partial(swap_kernel, bits, count),
        out_shape=(
            jax.ShapeDtypeStruct((2, 2) + low.shape, low.dtype),
            jax.ShapeDtypeStruct((count,) + low.shape, low.dtype),
        ),
        in_specs=[here] * 3,
        out_specs=(there, there),
        scratch_shapes=[
            pltpu.SemaphoreType.DMA((2,)),
            pltpu.SemaphoreType.DMA((2,)),
            pltpu.SemaphoreType.DMA((2,)),
            pltpu.SemaphoreType.DMA((2,)),
            pltpu.SemaphoreType.DMA((count,)),
            pltpu.SemaphoreType.DMA((count,)),
            pltpu.SemaphoreType.DMA,
        ],
        compiler_params=pltpu.CompilerParams(
            collective_id=bits // 2, has_side_effects=True, skip_device_barrier=True
        ),
    )(low, high, mine)


def whiten_kernel(limit_ref, x_ref, first_ref, twiddle_ref, second_ref, low_ref, high_ref, flat, spec):
    blocks, width, samples = x_ref.shape
    per = samples // SEG
    for j in range(blocks):
        for q in range(per):
            t1 = j * per + q
            flat[t1 * width : (t1 + 1) * width, :] = x_ref[
                j, :, q * SEG : (q + 1) * SEG
            ].astype(jnp.float32)
    cos, sin = twiddle_ref[0], twiddle_ref[1]
    for c in range(width):
        series = flat[pl.ds(c, R1, stride=width), :].astype(jnp.bfloat16)
        part = jnp.dot(first_ref[...], series, preferred_element_type=jnp.float32)
        real = part[:R1] + part[2 * R1 : 3 * R1]
        imag = part[R1 : 2 * R1] + part[3 * R1 :]
        turned = jnp.concatenate([real * cos + imag * sin, imag * cos - real * sin], axis=1)
        high = turned.astype(jnp.bfloat16)
        low = (turned - high.astype(jnp.float32)).astype(jnp.bfloat16)
        result = jnp.dot(high, second_ref[0], preferred_element_type=jnp.float32)
        result += jnp.dot(low, second_ref[0], preferred_element_type=jnp.float32)
        result += jnp.dot(high, second_ref[1], preferred_element_type=jnp.float32)
        spec[pl.ds(c, R1, stride=width), :] = result
    lane = lax.broadcasted_iota(jnp.int32, (width, 2 * R2), 1) % R2
    channel = lax.broadcasted_iota(jnp.int32, (width, 2 * R2), 0)
    alive = (channel < limit_ref[0]).astype(jnp.float32)
    power = []
    for kappa in range(R1):
        square = jnp.square(spec[kappa * width : (kappa + 1) * width, :])
        power.append(square + pltpu.roll(square, R2, 1))
    upto, total = [], None
    for kappa in range(R1):
        total = power[kappa] if total is None else total + power[kappa]
        upto.append(total)
    rest = None
    for kappa in reversed(range(R1)):
        rest = power[kappa] if rest is None else rest + power[kappa]
        below = jnp.where(lane == 0, 0.0, pltpu.roll(rest, 1, 1))
        above = jnp.where(lane == R2 - 1, 0.0, pltpu.roll(upto[kappa], 2 * R2 - 1, 1))
        smooth = (below + total + above) * (1.0 / (2 * WH + 1))
        factor = alive * lax.rsqrt(smooth + epsilon)
        piece = spec[kappa * width : (kappa + 1) * width, :] * factor
        half_ref = (low_ref, high_ref)[kappa // HALF]
        half_ref[kappa % HALF] = piece.astype(jnp.bfloat16)


def whiten(limit, x):
    first, twiddle, second = forward_constants()
    _, width, _ = x.shape
    rows = R1 * width
    vmem = pl.BlockSpec(memory_space=pltpu.VMEM)
    return pl.pallas_call(
        whiten_kernel,
        out_shape=(jax.ShapeDtypeStruct((HALF, width, 2 * R2), jnp.bfloat16),) * 2,
        in_specs=[pl.BlockSpec(memory_space=pltpu.SMEM)] + [vmem] * 4,
        out_specs=(vmem, vmem),
        scratch_shapes=[
            pltpu.VMEM((rows, SEG), jnp.float32),
            pltpu.VMEM((rows, 2 * R2), jnp.float32),
        ],
    )(
        limit,
        x,
        jnp.asarray(first, jnp.bfloat16),
        jnp.asarray(twiddle, jnp.float32),
        jnp.asarray(second, jnp.bfloat16),
    )


def correlate_kernel(partner_ref, low_ref, high_ref, *refs):
    rounds = len(refs) - 7
    their_refs = refs[:rounds]
    ta_ref, tb_ref, lag_ref, o_ref, aa, bb, ss = refs[rounds:]
    parts, _, width, lanes = low_ref.shape
    slots = [partner_ref[turn, 0] % 2 for turn in range(rounds)]
    channels = parts * width
    pairs = rounds * width

    def transform(p, carry):
        q = jnp.where(p == 0, 0, HALF - p)
        mine = [low_ref[:, p].reshape(channels, lanes), high_ref[:, q].reshape(channels, lanes)]
        mine = jnp.concatenate(mine, axis=1)
        part = lax.dot_general(
            ta_ref[p], mine, (((1,), (1,)), ((), ())), preferred_element_type=jnp.float32
        )
        their = [
            jnp.concatenate([ref[slot, 0, p], ref[slot, 1, q]], axis=1)
            for ref, slot in zip(their_refs, slots)
        ]
        their = jnp.concatenate(their + their, axis=0)
        other = lax.dot_general(
            tb_ref[p], their, (((1,), (1,)), ((), ())), preferred_element_type=jnp.float32
        )
        left = lax.broadcasted_iota(jnp.int32, (SEG, 2 * pairs), 1) < pairs
        for h in range(2):
            for e in range(2):
                row = pl.ds(pl.multiple_of(((2 * h + e) * HALF + p) * SEG, SEG), SEG)
                start = (2 * h + e) * SEG
                aa[row, :] = part[start : start + SEG]
            real = other[2 * h * SEG : (2 * h + 1) * SEG]
            imag = other[(2 * h + 1) * SEG : (2 * h + 2) * SEG]
            row = pl.ds(pl.multiple_of((2 * h * HALF + p) * SEG, SEG), SEG)
            bb[row, : 2 * pairs] = jnp.where(left, real, -imag)
            row = pl.ds(pl.multiple_of(((2 * h + 1) * HALF + p) * SEG, SEG), SEG)
            bb[row, : 2 * pairs] = jnp.where(left, imag, real)
        return carry

    lax.fori_loop(0, HALF, transform, 0)

    def multiply(f, carry):
        mine = aa[pl.ds(f, 2 * R1, stride=SEG), :].astype(jnp.bfloat16)
        their = bb[pl.ds(f, 2 * R1, stride=SEG), :].astype(jnp.bfloat16)[:, : 2 * pairs]
        product = lax.dot_general(
            their, mine, (((0,), (0,)), ((), ())), preferred_element_type=jnp.float32
        )
        start = pl.multiple_of(f * 2 * pairs, 2 * pairs)
        ss[pl.ds(start, 2 * pairs), :] = product
        return carry

    lax.fori_loop(0, SEG, multiply, 0, unroll=4)

    for turn in range(rounds):
        for b in range(width):
            piece = ss[pl.ds(turn * width + b, 2 * SEG, stride=pairs), :].astype(jnp.bfloat16)
            start = (b * rounds + turn) * channels
            o_ref[:, start : start + channels] = jnp.dot(
                lag_ref[...], piece, preferred_element_type=jnp.float32
            )


def correlate(partner, low, high, theirs):
    parts, _, width, lanes = low.shape
    channels = parts * width
    rounds = len(theirs)
    vmem = pl.BlockSpec(memory_space=pltpu.VMEM)
    return pl.pallas_call(
        correlate_kernel,
        out_shape=jax.ShapeDtypeStruct((LAGS, width * rounds * channels), jnp.float32),
        in_specs=[pl.BlockSpec(memory_space=pltpu.SMEM)] + [vmem] * (rounds + 5),
        out_specs=vmem,
        scratch_shapes=[
            pltpu.VMEM((4 * HALF * SEG, channels), jnp.float32),
            pltpu.VMEM((4 * HALF * SEG, 128), jnp.float32),
            pltpu.VMEM((SEG * 2 * rounds * width, channels), jnp.float32),
        ],
        compiler_params=pltpu.CompilerParams(vmem_limit_bytes=60 * 2**20),
    )(
        partner,
        low,
        high,
        *theirs,
        jnp.asarray(segment_table(-LAGS // 2, SEG + LAGS // 2), jnp.bfloat16),
        jnp.asarray(segment_table(0, SEG), jnp.bfloat16),
        jnp.asarray(lag_table(), jnp.bfloat16),
    )


def per_device(strain, dead_counts, partner):
    channels = strain.shape[0]
    count, blocks = lax.axis_size("tm"), lax.axis_size("chan")
    width = channels // count
    limit = channels - dead_counts - lax.axis_index("tm") * width
    halves = whiten(limit, scatter(strain, count, width))
    routes = [functools.partial(swap, bits, count) for bits in range(0, blocks, 2)]
    theirs, own = [], []
    for turn in range(partner.shape[0]):
        their, part = lax.switch(partner[turn, 0] // 2, routes, *halves, halves[turn])
        theirs.append(their)
        own.append(part)
    return correlate(partner, *own, theirs)


def solution(mesh):
    return jax.shard_map(
        per_device,
        mesh=mesh,
        in_specs=(P("chan", "tm"), P("chan"), P()),
        out_specs=P(None, ("chan", "tm")),
        check_vma=False,
    )
```

```python
import functools
import math

import jax
import jax.numpy as jnp
import numpy as np
from jax import lax
from jax.experimental import pallas as pl
from jax.experimental.pallas import tpu as pltpu
from jax.sharding import PartitionSpec as P

NF = 2048
WH = 32
LAGS = 128
NT = 4096
epsilon = 1e-05

R1 = 32
R2 = NF // R1
SEG = NT // R1
HALF = R1 // 2


def split_bf16(table):
    table = np.asarray(table, np.float32)
    high = table.astype(np.dtype(jnp.bfloat16)).astype(np.float32)
    return high, table - high


@functools.cache
def forward_constants():
    kappa, t1 = np.arange(R1), np.arange(R1)
    phase = 2 * np.pi * (kappa[:, None] * t1[None, :] % R1) / R1
    first = np.concatenate([np.cos(phase), -np.sin(phase)], axis=0)
    first = np.concatenate(split_bf16(first), axis=0)
    t0 = np.arange(SEG)
    phase = 2 * np.pi * (kappa[:, None] * t0[None, :]) / NT
    amplitude = 1 / math.sqrt(NT)
    twiddle = np.stack([np.cos(phase) * amplitude, np.sin(phase) * amplitude])
    k2 = np.arange(R2)
    phase = 2 * np.pi * (t0[:, None] * k2[None, :] % SEG) / SEG
    cos, sin = np.cos(phase), np.sin(phase)
    second = np.block([[cos, -sin], [sin, cos]])
    second = np.stack(split_bf16(second))
    return first.astype(np.float32), twiddle.astype(np.float32), second.astype(np.float32)


def window_sums(low, high):
    x = np.arange(-2 * NT, 2 * NT)
    u = np.arange(low, high)
    return np.exp(2j * np.pi * (x[:, None] * u[None, :] % NT) / NT).sum(1)


@functools.cache
def segment_table(low, high):
    sums = window_sums(low, high)
    f, k2 = np.arange(SEG), np.arange(R2)
    out = np.zeros((HALF + 1, 2, SEG, 2, 2, R2))
    for p in range(HALF + 1):
        classes = (p % HALF, R1 - p if p % HALF else HALF)
        for h, target in enumerate(classes):
            for g in range(2):
                if p % HALF:
                    source, mirrored = classes[g], g != h
                elif g == h and p == 0:
                    source, mirrored = target, False
                elif g != h and p == HALF:
                    source, mirrored = target, True
                else:
                    continue
                k = (-1 if mirrored else 1) * (source + R1 * k2)
                part = sums[k[None, :] - R1 // 2 * f[:, None] - R1 // 4 + 2 * NT]
                if source == 0:
                    part[:, 0] *= 0.0 if mirrored else math.sqrt(2.0)
                out[p, h, :, g, 0] = part.real
                out[p, h, :, g, 1] = part.imag if mirrored else -part.imag
    return out.reshape(HALF + 1, 2 * SEG, 4 * R2).astype(np.float32)


@functools.cache
def lag_table():
    tau, f = np.arange(LAGS) - LAGS // 2, np.arange(SEG)
    phase = 2 * np.pi * (f[None, :] + 0.5) * tau[:, None] / (2 * SEG)
    table = np.stack([np.cos(phase), -np.sin(phase)], axis=-1)
    scale = 1 / (2.0**19 * math.sqrt(2.0))
    return (table * scale).reshape(LAGS, 2 * SEG).astype(np.float32)


MESH = pl.DeviceIdType.MESH


def signal(**target):
    barrier = pltpu.get_barrier_semaphore()
    pl.semaphore_signal(barrier, inc=1, device_id=target, device_id_type=MESH)


def send(src, dst, sems, index, **target):
    copy = pltpu.make_async_remote_copy(
        src_ref=src,
        dst_ref=dst,
        send_sem=sems[0].at[index],
        recv_sem=sems[1].at[index],
        device_id=target,
        device_id_type=MESH,
    )
    copy.start()
    return copy


def scatter_kernel(count, width, x_ref, o_ref, send_sem, recv_sem, own_sem):
    me = lax.axis_index("tm")
    peers = [lax.rem(me + step, count) for step in range(1, count)]
    for peer in peers:
        signal(tm=peer)
    pl.semaphore_wait(pltpu.get_barrier_semaphore(), len(peers))

    def rows(index):
        return x_ref.at[pl.ds(pl.multiple_of(index * width, width), width), :]

    copies = [
        send(rows(peer), o_ref.at[me], (send_sem, recv_sem), step, tm=peer)
        for step, peer in enumerate(peers)
    ]
    own = pltpu.make_async_copy(rows(me), o_ref.at[me], own_sem)
    own.start()
    own.wait()
    for copy in copies:
        copy.wait()


def scatter(strain, count, width):
    return pl.pallas_call(
        functools.partial(scatter_kernel, count, width),
        out_shape=jax.ShapeDtypeStruct((count, width, strain.shape[1]), strain.dtype),
        in_specs=[pl.BlockSpec(memory_space=pltpu.VMEM)],
        out_specs=pl.BlockSpec(memory_space=pl.ANY),
        scratch_shapes=[
            pltpu.SemaphoreType.DMA((count,)),
            pltpu.SemaphoreType.DMA((count,)),
            pltpu.SemaphoreType.DMA,
        ],
        compiler_params=pltpu.CompilerParams(
            collective_id=32, has_side_effects=True, skip_device_barrier=True
        ),
    )(strain)


def swap_kernel(bits, count, low_ref, high_ref, mine_ref, their_ref, all_ref, *sems):
    pair_sems, over_sems, ring_sems, own_sem = sems[0:2], sems[2:4], sems[4:6], sems[6]
    me, block = lax.axis_index("tm"), lax.axis_index("chan")
    right, left = lax.rem(me + 2, count), lax.rem(me + count - 2, count)
    side = me + 1 - 2 * (me % 2)
    partner = block
    for digit in range(bits.bit_length()):
        if bits >> digit & 1:
            partner = partner + 2**digit * (1 - 2 * (block // 2**digit % 2))
    beside = block + 1 - 2 * (block % 2)
    for peer in (right, left, side):
        signal(tm=peer)
    signal(chan=beside)
    if bits:
        signal(chan=partner)
    pl.semaphore_wait(pltpu.get_barrier_semaphore(), 4 + (bits > 0))
    halves = (low_ref, high_ref)
    if bits:
        pair = [
            send(half, their_ref.at[0, h], pair_sems, h, chan=partner)
            for h, half in enumerate(halves)
        ]
    else:
        pair = [
            pltpu.make_async_copy(half, their_ref.at[0, h], pair_sems[0].at[h])
            for h, half in enumerate(halves)
        ]
        for copy in pair:
            copy.start()
    size = mine_ref.shape[0] // 2
    first, last = pl.ds(0, size), pl.ds(size, size)

    def onward(ref, index, peer):
        return send(ref, ref, ring_sems, index, tm=peer)

    to_side = send(mine_ref, all_ref.at[me], ring_sems, 2, tm=side)
    to_right = send(mine_ref, all_ref.at[me], ring_sems, 0, tm=right)
    to_left = send(mine_ref, all_ref.at[me], ring_sems, 1, tm=left)
    own = pltpu.make_async_copy(mine_ref, all_ref.at[me], own_sem)
    own.start()
    to_side.wait_recv()
    side_right = onward(all_ref.at[side], 3, right)
    side_left = onward(all_ref.at[side], 4, left)
    to_right.wait_recv()
    far_right = onward(all_ref.at[left, first], 5, right)
    to_left.wait_recv()
    far_left = onward(all_ref.at[right, last], 6, left)
    over = []
    for h, copy in enumerate(pair):
        if bits:
            copy.wait_recv()
        else:
            copy.wait()
        over.append(send(their_ref.at[0, h], their_ref.at[1, h], over_sems, h, chan=beside))
        if h == 0:
            side_right.wait_recv()
            step = left + 1 - 2 * (left % 2)
            far_side_right = onward(all_ref.at[step, first], 7, right)
            side_left.wait_recv()
            step = right + 1 - 2 * (right % 2)
            far_side_left = onward(all_ref.at[step, last], 8, left)
    for copy in (to_side, to_right, to_left, side_right, side_left):
        copy.wait_send()
    if bits:
        for copy in pair:
            copy.wait_send()
    own.wait()
    for copy in [far_right, far_left, far_side_right, far_side_left] + over:
        copy.wait()


def swap(bits, count, low, high, mine):
    here = pl.BlockSpec(memory_space=pltpu.VMEM)
    there = pl.BlockSpec(memory_space=pl.ANY)
    return pl.pallas_call(
        functools.partial(swap_kernel, bits, count),
        out_shape=(
            jax.ShapeDtypeStruct((2, 2) + low.shape, low.dtype),
            jax.ShapeDtypeStruct((count,) + low.shape, low.dtype),
        ),
        in_specs=[here] * 3,
        out_specs=(there, there),
        scratch_shapes=[
            pltpu.SemaphoreType.DMA((2,)),
            pltpu.SemaphoreType.DMA((2,)),
            pltpu.SemaphoreType.DMA((2,)),
            pltpu.SemaphoreType.DMA((2,)),
            pltpu.SemaphoreType.DMA((9,)),
            pltpu.SemaphoreType.DMA((9,)),
            pltpu.SemaphoreType.DMA,
        ],
        compiler_params=pltpu.CompilerParams(
            collective_id=bits // 2, has_side_effects=True, skip_device_barrier=True
        ),
    )(low, high, mine)


def whiten_kernel(
    count, dead_ref, partner_ref, x_ref, first_ref, twiddle_ref, second_ref, *refs
):
    low_ref, high_ref, *index_refs, flat, spec = refs
    for turn, index_ref in enumerate(index_refs):
        index_ref[0] = partner_ref[turn, 0] // 2
    blocks, width, samples = x_ref.shape
    step = flat.shape[0] // R1
    per = samples // SEG
    limit = count * width - dead_ref[0] - lax.axis_index("tm") * width
    for j in range(blocks):
        for q in range(per):
            start = (j * per + q) * step
            flat[start : start + width, :] = x_ref[j, :, q * SEG : (q + 1) * SEG].astype(
                jnp.float32
            )
    cos, sin = twiddle_ref[0], twiddle_ref[1]
    for c in range(width):
        series = flat[pl.ds(c, R1, stride=step), :].astype(jnp.bfloat16)
        part = jnp.dot(first_ref[...], series, preferred_element_type=jnp.float32)
        real = part[:R1] + part[2 * R1 : 3 * R1]
        imag = part[R1 : 2 * R1] + part[3 * R1 :]
        turned = jnp.concatenate([real * cos + imag * sin, imag * cos - real * sin], axis=1)
        high = turned.astype(jnp.bfloat16)
        low = (turned - high.astype(jnp.float32)).astype(jnp.bfloat16)
        result = jnp.dot(high, second_ref[0], preferred_element_type=jnp.float32)
        result += jnp.dot(low, second_ref[0], preferred_element_type=jnp.float32)
        result += jnp.dot(high, second_ref[1], preferred_element_type=jnp.float32)
        spec[pl.ds(c, R1, stride=step), :] = result
    lane = lax.broadcasted_iota(jnp.int32, (width, 2 * R2), 1) % R2
    channel = lax.broadcasted_iota(jnp.int32, (width, 2 * R2), 0)
    alive = (channel < limit).astype(jnp.float32)
    power = []
    for kappa in range(R1):
        square = jnp.square(spec[kappa * step : kappa * step + width, :])
        power.append(square + pltpu.roll(square, R2, 1))
    upto, total = [], None
    for kappa in range(R1):
        total = power[kappa] if total is None else total + power[kappa]
        upto.append(total)
    rest = None
    for kappa in reversed(range(R1)):
        rest = power[kappa] if rest is None else rest + power[kappa]
        below = jnp.where(lane == 0, 0.0, pltpu.roll(rest, 1, 1))
        above = jnp.where(lane == R2 - 1, 0.0, pltpu.roll(upto[kappa], 2 * R2 - 1, 1))
        smooth = (below + total + above) * (1.0 / (2 * WH + 1))
        factor = alive * lax.rsqrt(smooth + epsilon)
        piece = spec[kappa * step : kappa * step + width, :] * factor
        half_ref = (low_ref, high_ref)[kappa // HALF]
        half_ref[kappa % HALF] = piece.astype(jnp.bfloat16)


def whiten(dead_counts, partner, x):
    first, twiddle, second = forward_constants()
    count, width, _ = x.shape
    rounds = partner.shape[0]
    rows = R1 * (width + 8)
    vmem = pl.BlockSpec(memory_space=pltpu.VMEM)
    smem = pl.BlockSpec(memory_space=pltpu.SMEM)
    return pl.pallas_call(
        functools.partial(whiten_kernel, count),
        out_shape=(jax.ShapeDtypeStruct((HALF, width, 2 * R2), jnp.bfloat16),) * 2
        + (jax.ShapeDtypeStruct((1,), jnp.int32),) * rounds,
        in_specs=[smem] * 2 + [vmem] * 4,
        out_specs=(vmem, vmem) + (smem,) * rounds,
        scratch_shapes=[
            pltpu.VMEM((rows, SEG), jnp.float32),
            pltpu.VMEM((rows, 2 * R2), jnp.float32),
        ],
    )(
        dead_counts,
        partner,
        x,
        jnp.asarray(first, jnp.bfloat16),
        jnp.asarray(twiddle, jnp.float32),
        jnp.asarray(second, jnp.bfloat16),
    )


def quarter_turn(panel):
    lanes = panel.shape[1]
    wide = pltpu.roll(panel.astype(jnp.float32), lanes // 2, 1)
    left = lax.broadcasted_iota(jnp.int32, panel.shape, 1) < lanes // 2
    return jnp.where(left, wide, -wide).astype(jnp.bfloat16)


def correlate_kernel(partner_ref, low_ref, high_ref, *refs):
    rounds = len(refs) - 7
    their_refs = refs[:rounds]
    ta_ref, tb_ref, lag_ref, o_ref, aa, bb, ss = refs[rounds:]
    parts, _, width, lanes = low_ref.shape
    channels = parts * width
    pairs = rounds * width
    step = aa.shape[0] // (2 * R1)
    slots = [partner_ref[turn, 0] % 2 for turn in range(rounds)]

    def times(table, panel):
        return lax.dot_general(
            table, panel, (((1,), (1,)), ((), ())), preferred_element_type=jnp.float32
        )

    def panels(p, q):
        mine = [low_ref[:, p].reshape(channels, lanes), high_ref[:, q].reshape(channels, lanes)]
        their = [
            jnp.concatenate([ref[slot, half, k] for ref, slot in zip(their_refs, slots)], axis=0)
            for half, k in ((0, p), (1, q))
        ]
        return [(side, quarter_turn(side)) for side in mine + their]

    def products(index, mine, their):
        (one, turned_one), (two, turned_two) = mine
        rows = [[one, two], [turned_one, -turned_two]]
        part = times(
            ta_ref[index], jnp.concatenate([jnp.concatenate(r, axis=1) for r in rows], axis=0)
        )
        (one, turned_one), (two, turned_two) = their
        rows = [[one, two], [-turned_one, turned_two], [turned_one, -turned_two], [one, two]]
        other = times(
            tb_ref[index], jnp.concatenate([jnp.concatenate(r, axis=1) for r in rows], axis=0)
        )
        return part, other

    group = lax.broadcasted_iota(jnp.int32, (SEG, 4 * pairs), 1) // pairs
    odd = group % 2 == 1

    def keep(p, part, other):
        for h in range(2):
            rows = slice(h * SEG, (h + 1) * SEG)
            for e in range(2):
                start = pl.multiple_of((2 * HALF * e + HALF * h + p) * step, 8)
                aa[pl.ds(start, SEG), :] = part[rows, e * channels : (e + 1) * channels]
            start = pl.multiple_of((HALF * h + p) * step, 8)
            kept = other[rows]
            bb[pl.ds(start, SEG), :] = jnp.where(odd, -kept, kept) if h else kept

    ends = panels(0, 0)
    part, other = products(0, ends[:2], ends[2:])
    mirrored, mirrored_other = products(HALF, ends[1::-1], ends[:1:-1])
    keep(0, part + mirrored, other + mirrored_other)

    def transform(p, carry):
        sides = panels(p, HALF - p)
        keep(p, *products(p, sides[:2], sides[2:]))
        return carry

    lax.fori_loop(1, HALF, transform, 0, unroll=3)
    gap = ss.shape[0] // (2 * SEG)

    def multiply(f, carry):
        mine = aa[pl.ds(f, 2 * R1, stride=step), :].astype(jnp.bfloat16)
        their = bb[pl.ds(f, R1, stride=step), :]
        their = jnp.concatenate([their[:, : 2 * pairs], their[:, 2 * pairs :]], axis=0)
        product = lax.dot_general(
            their.astype(jnp.bfloat16),
            mine,
            (((0,), (0,)), ((), ())),
            preferred_element_type=jnp.float32,
        )
        for part in range(2):
            start = pl.multiple_of((2 * f + part) * gap, 8)
            ss[pl.ds(start, pairs), :] = product[part * pairs : (part + 1) * pairs]
        return carry

    lax.fori_loop(0, SEG, multiply, 0, unroll=8)

    for b in range(width):
        pieces = [
            ss[pl.ds(turn * width + b, 2 * SEG, stride=gap), :].astype(jnp.bfloat16)
            for turn in range(rounds)
        ]
        start = b * rounds * channels
        o_ref[:, start : start + rounds * channels] = jnp.dot(
            lag_ref[...], jnp.concatenate(pieces, axis=1), preferred_element_type=jnp.float32
        )


def correlate(partner, low, high, theirs):
    parts, _, width, lanes = low.shape
    channels = parts * width
    rounds = len(theirs)
    vmem = pl.BlockSpec(memory_space=pltpu.VMEM)
    return pl.pallas_call(
        correlate_kernel,
        out_shape=jax.ShapeDtypeStruct((LAGS, width * rounds * channels), jnp.float32),
        in_specs=[pl.BlockSpec(memory_space=pltpu.SMEM)] + [vmem] * (rounds + 5),
        out_specs=vmem,
        scratch_shapes=[
            pltpu.VMEM((2 * R1 * (SEG + 8), channels), jnp.float32),
            pltpu.VMEM((R1 * (SEG + 8), 4 * rounds * width), jnp.float32),
            pltpu.VMEM((2 * SEG * (rounds * width + 8), channels), jnp.float32),
        ],
        compiler_params=pltpu.CompilerParams(vmem_limit_bytes=60 * 2**20),
    )(
        partner,
        low,
        high,
        *theirs,
        jnp.asarray(segment_table(-LAGS // 2, SEG + LAGS // 2), jnp.bfloat16),
        jnp.asarray(segment_table(0, SEG), jnp.bfloat16),
        jnp.asarray(lag_table(), jnp.bfloat16),
    )


def per_device(strain, dead_counts, partner):
    channels = strain.shape[0]
    count, blocks = lax.axis_size("tm"), lax.axis_size("chan")
    width = channels // count
    low, high, *indices = whiten(dead_counts, partner, scatter(strain, count, width))
    routes = [functools.partial(swap, bits, count) for bits in range(0, blocks, 2)]
    theirs, own = [], []
    for mine, index in zip((low, high), indices):
        their, part = lax.switch(index[0], routes, low, high, mine)
        theirs.append(their)
        own.append(part)
    return correlate(partner, *own, theirs)


def solution(mesh):
    return jax.shard_map(
        per_device,
        mesh=mesh,
        in_specs=(P("chan", "tm"), P("chan"), P()),
        out_specs=P(None, ("chan", "tm")),
        check_vma=False,
    )
```

```python
import functools
import math

import jax
import jax.numpy as jnp
import numpy as np
from jax import lax
from jax.experimental import pallas as pl
from jax.experimental.pallas import tpu as pltpu
from jax.sharding import PartitionSpec as P

NF = 2048
WH = 32
LAGS = 128
NT = 4096
epsilon = 1e-05

R1 = 32
R2 = NF // R1
SEG = NT // R1
HALF = R1 // 2


def split_bf16(table):
    table = np.asarray(table, np.float32)
    high = table.astype(np.dtype(jnp.bfloat16)).astype(np.float32)
    return high, table - high


@functools.cache
def forward_constants():
    kappa, t1 = np.arange(R1), np.arange(R1)
    phase = 2 * np.pi * (kappa[:, None] * t1[None, :] % R1) / R1
    first = np.concatenate([np.cos(phase), -np.sin(phase)], axis=0)
    first = np.concatenate(split_bf16(first), axis=0)
    t0 = np.arange(SEG)
    phase = 2 * np.pi * (kappa[:, None] * t0[None, :]) / NT
    amplitude = 1 / math.sqrt(NT)
    twiddle = np.stack([np.cos(phase) * amplitude, np.sin(phase) * amplitude])
    k2 = np.arange(R2)
    phase = 2 * np.pi * (t0[:, None] * k2[None, :] % SEG) / SEG
    cos, sin = np.cos(phase), np.sin(phase)
    second = np.block([[cos, -sin], [sin, cos]])
    second = np.stack(split_bf16(second))
    return first.astype(np.float32), twiddle.astype(np.float32), second.astype(np.float32)


def window_sums(low, high):
    x = np.arange(-2 * NT, 2 * NT)
    u = np.arange(low, high)
    return np.exp(2j * np.pi * (x[:, None] * u[None, :] % NT) / NT).sum(1)


@functools.cache
def segment_table(low, high):
    sums = window_sums(low, high)
    f, k2 = np.arange(SEG), np.arange(R2)
    out = np.zeros((HALF + 1, 2, SEG, 2, 2, R2))
    for p in range(HALF + 1):
        classes = (p % HALF, R1 - p if p % HALF else HALF)
        for h, target in enumerate(classes):
            for g in range(2):
                if p % HALF:
                    source, mirrored = classes[g], g != h
                elif g == h and p == 0:
                    source, mirrored = target, False
                elif g != h and p == HALF:
                    source, mirrored = target, True
                else:
                    continue
                k = (-1 if mirrored else 1) * (source + R1 * k2)
                part = sums[k[None, :] - R1 // 2 * f[:, None] - R1 // 4 + 2 * NT]
                if source == 0:
                    part[:, 0] *= 0.0 if mirrored else math.sqrt(2.0)
                out[p, h, :, g, 0] = part.real
                out[p, h, :, g, 1] = part.imag if mirrored else -part.imag
    return out.reshape(HALF + 1, 2 * SEG, 4 * R2).astype(np.float32)


@functools.cache
def lag_table():
    tau, f = np.arange(LAGS) - LAGS // 2, np.arange(SEG)
    phase = 2 * np.pi * (f[None, :] + 0.5) * tau[:, None] / (2 * SEG)
    table = np.stack([np.cos(phase), -np.sin(phase)], axis=-1)
    scale = 1 / (2.0**19 * math.sqrt(2.0))
    return (table * scale).reshape(LAGS, 2 * SEG).astype(np.float32)


MESH = pl.DeviceIdType.MESH


def signal(**target):
    barrier = pltpu.get_barrier_semaphore()
    pl.semaphore_signal(barrier, inc=1, device_id=target, device_id_type=MESH)


def send(src, dst, sems, index, **target):
    copy = pltpu.make_async_remote_copy(
        src_ref=src,
        dst_ref=dst,
        send_sem=sems[0].at[index],
        recv_sem=sems[1].at[index],
        device_id=target,
        device_id_type=MESH,
    )
    copy.start()
    return copy


def scatter_kernel(count, width, x_ref, o_ref, send_sem, recv_sem, own_sem):
    me = lax.axis_index("tm")
    peers = [lax.rem(me + step, count) for step in range(1, count)]
    for peer in peers:
        signal(tm=peer)
    pl.semaphore_wait(pltpu.get_barrier_semaphore(), len(peers))

    def rows(index):
        return x_ref.at[pl.ds(pl.multiple_of(index * width, width), width), :]

    copies = [
        send(rows(peer), o_ref.at[me], (send_sem, recv_sem), step, tm=peer)
        for step, peer in enumerate(peers)
    ]
    own = pltpu.make_async_copy(rows(me), o_ref.at[me], own_sem)
    own.start()
    own.wait()
    for copy in copies:
        copy.wait()


def scatter(strain, count, width):
    return pl.pallas_call(
        functools.partial(scatter_kernel, count, width),
        out_shape=jax.ShapeDtypeStruct((count, width, strain.shape[1]), strain.dtype),
        in_specs=[pl.BlockSpec(memory_space=pltpu.VMEM)],
        out_specs=pl.BlockSpec(memory_space=pl.ANY),
        scratch_shapes=[
            pltpu.SemaphoreType.DMA((count,)),
            pltpu.SemaphoreType.DMA((count,)),
            pltpu.SemaphoreType.DMA,
        ],
        compiler_params=pltpu.CompilerParams(
            collective_id=32, has_side_effects=True, skip_device_barrier=True
        ),
    )(strain)


def beside_kernel(rounds, partner_ref, x_ref, *refs):
    out_refs, got, send_sem, recv_sem = refs[:rounds], *refs[rounds:]
    block = lax.axis_index("chan")
    beside = block + 1 - 2 * (block % 2)
    signal(chan=beside)
    pl.semaphore_wait(pltpu.get_barrier_semaphore(), 1)
    copy = send(x_ref, got, (send_sem, recv_sem), 0, chan=beside)
    copy.wait()
    for turn, out_ref in enumerate(out_refs):
        out_ref[...] = jnp.where(partner_ref[turn, 0] % 2 == 1, got[...], x_ref[...])


def pick_core(partner, piece):
    rounds = partner.shape[0]
    vmem = pl.BlockSpec(memory_space=pltpu.VMEM)
    return pl.pallas_call(
        functools.partial(beside_kernel, rounds),
        out_shape=(jax.ShapeDtypeStruct(piece.shape, piece.dtype),) * rounds,
        in_specs=[pl.BlockSpec(memory_space=pltpu.SMEM), vmem],
        out_specs=(vmem,) * rounds,
        scratch_shapes=[
            pltpu.VMEM(piece.shape, piece.dtype),
            pltpu.SemaphoreType.DMA((1,)),
            pltpu.SemaphoreType.DMA((1,)),
        ],
        compiler_params=pltpu.CompilerParams(
            collective_id=33, has_side_effects=True, skip_device_barrier=True
        ),
    )(partner, piece)


def gather_kernel(count, mine_ref, all_ref, *sems):
    ring_sems, own_sem = sems[:2], sems[2]
    me = lax.axis_index("tm")
    right, left = lax.rem(me + 2, count), lax.rem(me + count - 2, count)
    side = me + 1 - 2 * (me % 2)
    for peer in (right, left, side):
        signal(tm=peer)
    pl.semaphore_wait(pltpu.get_barrier_semaphore(), 3)
    size = mine_ref.shape[0] // 2
    first, last = pl.ds(0, size), pl.ds(size, size)

    def onward(ref, index, peer):
        return send(ref, ref, ring_sems, index, tm=peer)

    to_side = send(mine_ref, all_ref.at[me], ring_sems, 2, tm=side)
    to_right = send(mine_ref, all_ref.at[me], ring_sems, 0, tm=right)
    to_left = send(mine_ref, all_ref.at[me], ring_sems, 1, tm=left)
    own = pltpu.make_async_copy(mine_ref, all_ref.at[me], own_sem)
    own.start()
    to_side.wait_recv()
    side_right = onward(all_ref.at[side], 3, right)
    side_left = onward(all_ref.at[side], 4, left)
    to_right.wait_recv()
    far_right = onward(all_ref.at[left, first], 5, right)
    to_left.wait_recv()
    far_left = onward(all_ref.at[right, last], 6, left)
    side_right.wait_recv()
    step = left + 1 - 2 * (left % 2)
    far_side_right = onward(all_ref.at[step, first], 7, right)
    side_left.wait_recv()
    step = right + 1 - 2 * (right % 2)
    far_side_left = onward(all_ref.at[step, last], 8, left)
    for copy in (to_side, to_right, to_left, side_right, side_left):
        copy.wait_send()
    own.wait()
    for copy in (far_right, far_left, far_side_right, far_side_left):
        copy.wait()


def gather(piece, count):
    size = piece.size * 2
    return pl.pallas_call(
        functools.partial(gather_kernel, count),
        out_shape=jax.ShapeDtypeStruct((count,) + piece.shape, piece.dtype),
        in_specs=[pl.BlockSpec(memory_space=pltpu.VMEM)],
        out_specs=pl.BlockSpec(memory_space=pl.ANY),
        scratch_shapes=[
            pltpu.SemaphoreType.DMA((9,)),
            pltpu.SemaphoreType.DMA((9,)),
            pltpu.SemaphoreType.DMA,
        ],
        compiler_params=pltpu.CompilerParams(
            collective_id=34, has_side_effects=True, skip_device_barrier=True
        ),
        cost_estimate=pl.CostEstimate(
            flops=0, transcendentals=0, bytes_accessed=32 * count * size
        ),
    )(piece)


def whiten_kernel(
    count, dead_ref, partner_ref, x_ref, first_ref, twiddle_ref, second_ref, *refs
):
    o_ref, *index_refs, flat, spec = refs
    for turn, index_ref in enumerate(index_refs):
        index_ref[0] = partner_ref[turn, 0] // 2
    blocks, width, samples = x_ref.shape
    step = flat.shape[0] // R1
    per = samples // SEG
    limit = count * width - dead_ref[0] - lax.axis_index("tm") * width
    for j in range(blocks):
        for q in range(per):
            start = (j * per + q) * step
            flat[start : start + width, :] = x_ref[j, :, q * SEG : (q + 1) * SEG].astype(
                jnp.float32
            )
    cos, sin = twiddle_ref[0], twiddle_ref[1]
    for c in range(width):
        series = flat[pl.ds(c, R1, stride=step), :].astype(jnp.bfloat16)
        part = jnp.dot(first_ref[...], series, preferred_element_type=jnp.float32)
        real = part[:R1] + part[2 * R1 : 3 * R1]
        imag = part[R1 : 2 * R1] + part[3 * R1 :]
        turned = jnp.concatenate([real * cos + imag * sin, imag * cos - real * sin], axis=1)
        high = turned.astype(jnp.bfloat16)
        low = (turned - high.astype(jnp.float32)).astype(jnp.bfloat16)
        result = jnp.dot(high, second_ref[0], preferred_element_type=jnp.float32)
        result += jnp.dot(low, second_ref[0], preferred_element_type=jnp.float32)
        result += jnp.dot(high, second_ref[1], preferred_element_type=jnp.float32)
        spec[pl.ds(c, R1, stride=step), :] = result
    lane = lax.broadcasted_iota(jnp.int32, (width, 2 * R2), 1) % R2
    channel = lax.broadcasted_iota(jnp.int32, (width, 2 * R2), 0)
    alive = (channel < limit).astype(jnp.float32)
    power = []
    for kappa in range(R1):
        square = jnp.square(spec[kappa * step : kappa * step + width, :])
        power.append(square + pltpu.roll(square, R2, 1))
    upto, total = [], None
    for kappa in range(R1):
        total = power[kappa] if total is None else total + power[kappa]
        upto.append(total)
    rest = None
    for kappa in reversed(range(R1)):
        rest = power[kappa] if rest is None else rest + power[kappa]
        below = jnp.where(lane == 0, 0.0, pltpu.roll(rest, 1, 1))
        above = jnp.where(lane == R2 - 1, 0.0, pltpu.roll(upto[kappa], 2 * R2 - 1, 1))
        smooth = (below + total + above) * (1.0 / (2 * WH + 1))
        factor = alive * lax.rsqrt(smooth + epsilon)
        piece = spec[kappa * step : kappa * step + width, :] * factor
        o_ref[kappa] = piece.astype(jnp.bfloat16)


def whiten(dead_counts, partner, x):
    first, twiddle, second = forward_constants()
    count, width, _ = x.shape
    rounds = partner.shape[0]
    rows = R1 * (width + 8)
    vmem = pl.BlockSpec(memory_space=pltpu.VMEM)
    smem = pl.BlockSpec(memory_space=pltpu.SMEM)
    return pl.pallas_call(
        functools.partial(whiten_kernel, count),
        out_shape=(jax.ShapeDtypeStruct((R1, width, 2 * R2), jnp.bfloat16),)
        + (jax.ShapeDtypeStruct((1,), jnp.int32),) * rounds,
        in_specs=[smem] * 2 + [vmem] * 4,
        out_specs=(vmem,) + (smem,) * rounds,
        scratch_shapes=[
            pltpu.VMEM((rows, SEG), jnp.float32),
            pltpu.VMEM((rows, 2 * R2), jnp.float32),
        ],
    )(
        dead_counts,
        partner,
        x,
        jnp.asarray(first, jnp.bfloat16),
        jnp.asarray(twiddle, jnp.float32),
        jnp.asarray(second, jnp.bfloat16),
    )


def quarter_turn(panel):
    lanes = panel.shape[1]
    wide = pltpu.roll(panel.astype(jnp.float32), lanes // 2, 1)
    left = lax.broadcasted_iota(jnp.int32, panel.shape, 1) < lanes // 2
    return jnp.where(left, wide, -wide).astype(jnp.bfloat16)


def correlate_kernel(own_ref, *refs):
    rounds = len(refs) - 7
    their_refs = refs[:rounds]
    ta_ref, tb_ref, lag_ref, o_ref, aa, bb, ss = refs[rounds:]
    parts, _, width, lanes = own_ref.shape
    channels = parts * width
    pairs = rounds * width
    step = aa.shape[0] // (2 * R1)

    def times(table, panel):
        return lax.dot_general(
            table, panel, (((1,), (1,)), ((), ())), preferred_element_type=jnp.float32
        )

    def panels(*classes):
        mine = [own_ref[:, k].reshape(channels, lanes) for k in classes]
        their = [jnp.concatenate([ref[k] for ref in their_refs], axis=0) for k in classes]
        return [(side, quarter_turn(side)) for side in mine + their]

    def products(index, mine, their):
        (one, turned_one), (two, turned_two) = mine
        rows = [[one, two], [turned_one, -turned_two]]
        part = times(
            ta_ref[index], jnp.concatenate([jnp.concatenate(r, axis=1) for r in rows], axis=0)
        )
        (one, turned_one), (two, turned_two) = their
        rows = [[one, two], [-turned_one, turned_two], [turned_one, -turned_two], [one, two]]
        other = times(
            tb_ref[index], jnp.concatenate([jnp.concatenate(r, axis=1) for r in rows], axis=0)
        )
        return part, other

    group = lax.broadcasted_iota(jnp.int32, (SEG, 4 * pairs), 1) // pairs
    odd = group % 2 == 1

    def keep(p, part, other):
        for h in range(2):
            rows = slice(h * SEG, (h + 1) * SEG)
            for e in range(2):
                start = pl.multiple_of((2 * HALF * e + HALF * h + p) * step, 8)
                aa[pl.ds(start, SEG), :] = part[rows, e * channels : (e + 1) * channels]
            start = pl.multiple_of((HALF * h + p) * step, 8)
            kept = other[rows]
            bb[pl.ds(start, SEG), :] = jnp.where(odd, -kept, kept) if h else kept

    ends = panels(0, HALF)
    part, other = products(0, ends[:2], ends[2:])
    mirrored, mirrored_other = products(HALF, ends[1::-1], ends[:1:-1])
    keep(0, part + mirrored, other + mirrored_other)

    def transform(p, carry):
        sides = panels(p, R1 - p)
        keep(p, *products(p, sides[:2], sides[2:]))
        return carry

    lax.fori_loop(1, HALF, transform, 0, unroll=3)
    gap = ss.shape[0] // (2 * SEG)

    def multiply(f, carry):
        mine = aa[pl.ds(f, 2 * R1, stride=step), :].astype(jnp.bfloat16)
        their = bb[pl.ds(f, R1, stride=step), :]
        their = jnp.concatenate([their[:, : 2 * pairs], their[:, 2 * pairs :]], axis=0)
        product = lax.dot_general(
            their.astype(jnp.bfloat16),
            mine,
            (((0,), (0,)), ((), ())),
            preferred_element_type=jnp.float32,
        )
        for part in range(2):
            start = pl.multiple_of((2 * f + part) * gap, 8)
            ss[pl.ds(start, pairs), :] = product[part * pairs : (part + 1) * pairs]
        return carry

    lax.fori_loop(0, SEG, multiply, 0, unroll=8)

    for b in range(width):
        pieces = [
            ss[pl.ds(turn * width + b, 2 * SEG, stride=gap), :].astype(jnp.bfloat16)
            for turn in range(rounds)
        ]
        start = b * rounds * channels
        o_ref[:, start : start + rounds * channels] = jnp.dot(
            lag_ref[...], jnp.concatenate(pieces, axis=1), preferred_element_type=jnp.float32
        )


def correlate(own, theirs):
    parts, _, width, lanes = own.shape
    channels = parts * width
    rounds = len(theirs)
    vmem = pl.BlockSpec(memory_space=pltpu.VMEM)
    return pl.pallas_call(
        correlate_kernel,
        out_shape=jax.ShapeDtypeStruct((LAGS, width * rounds * channels), jnp.float32),
        in_specs=[vmem] * (rounds + 4),
        out_specs=vmem,
        scratch_shapes=[
            pltpu.VMEM((2 * R1 * (SEG + 8), channels), jnp.float32),
            pltpu.VMEM((R1 * (SEG + 8), 4 * rounds * width), jnp.float32),
            pltpu.VMEM((2 * SEG * (rounds * width + 8), channels), jnp.float32),
        ],
        compiler_params=pltpu.CompilerParams(vmem_limit_bytes=60 * 2**20),
    )(
        own,
        *theirs,
        jnp.asarray(segment_table(-LAGS // 2, SEG + LAGS // 2), jnp.bfloat16),
        jnp.asarray(segment_table(0, SEG), jnp.bfloat16),
        jnp.asarray(lag_table(), jnp.bfloat16),
    )


def permuted(bits, count, piece):
    if not bits:
        return piece
    return lax.ppermute(piece, "chan", [(i, i ^ bits) for i in range(count)])


def per_device(strain, dead_counts, partner):
    channels = strain.shape[0]
    count, blocks = lax.axis_size("tm"), lax.axis_size("chan")
    width = channels // count
    piece, *indices = whiten(dead_counts, partner, scatter(strain, count, width))
    sent = pick_core(partner, piece)

    def route(bits, turn):
        def branch(mine, held):
            their = permuted(bits, blocks, held)
            return (their, gather(mine, count)) if turn == 0 else (their,)

        return branch

    theirs, own = [], None
    for turn, (index, held) in enumerate(zip(indices, sent)):
        routes = [route(bits, turn) for bits in range(0, blocks, 2)]
        their, *rest = lax.switch(index[0], routes, piece, held)
        theirs.append(their)
        own = rest[0] if rest else own
    return correlate(own, theirs)


def solution(mesh):
    return jax.shard_map(
        per_device,
        mesh=mesh,
        in_specs=(P("chan", "tm"), P("chan"), P()),
        out_specs=P(None, ("chan", "tm")),
        check_vma=False,
    )
```

```python
import functools
import math

import jax
import jax.numpy as jnp
import numpy as np
from jax import lax
from jax.experimental import pallas as pl
from jax.experimental.pallas import tpu as pltpu
from jax.sharding import PartitionSpec as P

NF = 2048
WH = 32
LAGS = 128
NT = 4096
epsilon = 1e-05

R1 = 32
R2 = NF // R1
SEG = NT // R1
HALF = R1 // 2


def split_bf16(table):
    table = np.asarray(table, np.float32)
    high = table.astype(np.dtype(jnp.bfloat16)).astype(np.float32)
    return high, table - high


@functools.cache
def forward_constants():
    kappa, t1 = np.arange(R1), np.arange(R1)
    phase = 2 * np.pi * (kappa[:, None] * t1[None, :] % R1) / R1
    first = np.concatenate([np.cos(phase), -np.sin(phase)], axis=0)
    first = np.concatenate(split_bf16(first), axis=0)
    t0 = np.arange(SEG)
    phase = 2 * np.pi * (kappa[:, None] * t0[None, :]) / NT
    amplitude = 1 / math.sqrt(NT)
    twiddle = np.stack([np.cos(phase) * amplitude, np.sin(phase) * amplitude])
    k2 = np.arange(R2)
    phase = 2 * np.pi * (t0[:, None] * k2[None, :] % SEG) / SEG
    cos, sin = np.cos(phase), np.sin(phase)
    second = np.block([[cos, -sin], [sin, cos]])
    second = np.concatenate(split_bf16(second), axis=1)
    return first.astype(np.float32), twiddle.astype(np.float32), second.astype(np.float32)


def window_sums(low, high):
    x = np.arange(-2 * NT, 2 * NT)
    u = np.arange(low, high)
    return np.exp(2j * np.pi * (x[:, None] * u[None, :] % NT) / NT).sum(1)


@functools.cache
def segment_table(low, high):
    sums = window_sums(low, high)
    f, k2 = np.arange(SEG), np.arange(R2)
    out = np.zeros((HALF + 1, 2, SEG, 2, 2, R2))
    for p in range(HALF + 1):
        classes = (p % HALF, R1 - p if p % HALF else HALF)
        for h, target in enumerate(classes):
            for g in range(2):
                if p % HALF:
                    source, mirrored = classes[g], g != h
                elif g == h and p == 0:
                    source, mirrored = target, False
                elif g != h and p == HALF:
                    source, mirrored = target, True
                else:
                    continue
                k = (-1 if mirrored else 1) * (source + R1 * k2)
                part = sums[k[None, :] - R1 // 2 * f[:, None] - R1 // 4 + 2 * NT]
                if source == 0:
                    part[:, 0] *= 0.0 if mirrored else math.sqrt(2.0)
                out[p, h, :, g, 0] = part.real
                out[p, h, :, g, 1] = part.imag if mirrored else -part.imag
    return out.reshape(HALF + 1, 2 * SEG, 4 * R2).astype(np.float32)


@functools.cache
def lag_table():
    tau, f = np.arange(LAGS) - LAGS // 2, np.arange(SEG)
    phase = 2 * np.pi * (f[None, :] + 0.5) * tau[:, None] / (2 * SEG)
    table = np.stack([np.cos(phase), -np.sin(phase)], axis=-1)
    scale = 1 / (2.0**19 * math.sqrt(2.0))
    return (table * scale).reshape(LAGS, 2 * SEG).astype(np.float32)


MESH = pl.DeviceIdType.MESH


def signal(**target):
    barrier = pltpu.get_barrier_semaphore()
    pl.semaphore_signal(barrier, inc=1, device_id=target, device_id_type=MESH)


def send(src, dst, sems, index, **target):
    copy = pltpu.make_async_remote_copy(
        src_ref=src,
        dst_ref=dst,
        send_sem=sems[0].at[index],
        recv_sem=sems[1].at[index],
        device_id=target,
        device_id_type=MESH,
    )
    copy.start()
    return copy


def scatter_kernel(count, width, x_ref, o_ref, send_sem, recv_sem, own_sem):
    me = lax.axis_index("tm")
    peers = [lax.rem(me + step, count) for step in range(1, count)]
    for peer in peers:
        signal(tm=peer)
    pl.semaphore_wait(pltpu.get_barrier_semaphore(), len(peers))

    def rows(index):
        return x_ref.at[pl.ds(pl.multiple_of(index * width, width), width), :]

    copies = [
        send(rows(peer), o_ref.at[me], (send_sem, recv_sem), step, tm=peer)
        for step, peer in enumerate(peers)
    ]
    own = pltpu.make_async_copy(rows(me), o_ref.at[me], own_sem)
    own.start()
    own.wait()
    for copy in copies:
        copy.wait()


def scatter(strain, count, width):
    return pl.pallas_call(
        functools.partial(scatter_kernel, count, width),
        out_shape=jax.ShapeDtypeStruct((count, width, strain.shape[1]), strain.dtype),
        in_specs=[pl.BlockSpec(memory_space=pltpu.VMEM)],
        out_specs=pl.BlockSpec(memory_space=pl.ANY),
        scratch_shapes=[
            pltpu.SemaphoreType.DMA((count,)),
            pltpu.SemaphoreType.DMA((count,)),
            pltpu.SemaphoreType.DMA,
        ],
        compiler_params=pltpu.CompilerParams(
            collective_id=32, has_side_effects=True, skip_device_barrier=True
        ),
    )(strain)


def beside_kernel(rounds, partner_ref, x_ref, *refs):
    out_refs, got, send_sem, recv_sem = refs[:rounds], *refs[rounds:]
    block = lax.axis_index("chan")
    beside = block + 1 - 2 * (block % 2)
    signal(chan=beside)
    pl.semaphore_wait(pltpu.get_barrier_semaphore(), 1)
    copy = send(x_ref, got, (send_sem, recv_sem), 0, chan=beside)
    copy.wait()
    for turn, out_ref in enumerate(out_refs):
        out_ref[...] = jnp.where(partner_ref[turn, 0] % 2 == 1, got[...], x_ref[...])


def pick_core(partner, piece):
    rounds = partner.shape[0]
    vmem = pl.BlockSpec(memory_space=pltpu.VMEM)
    return pl.pallas_call(
        functools.partial(beside_kernel, rounds),
        out_shape=(jax.ShapeDtypeStruct(piece.shape, piece.dtype),) * rounds,
        in_specs=[pl.BlockSpec(memory_space=pltpu.SMEM), vmem],
        out_specs=(vmem,) * rounds,
        scratch_shapes=[
            pltpu.VMEM(piece.shape, piece.dtype),
            pltpu.SemaphoreType.DMA((1,)),
            pltpu.SemaphoreType.DMA((1,)),
        ],
        compiler_params=pltpu.CompilerParams(
            collective_id=33, has_side_effects=True, skip_device_barrier=True
        ),
    )(partner, piece)


def gather_kernel(count, mine_ref, all_ref, *sems):
    ring_sems, own_sem = sems[:2], sems[2]
    me = lax.axis_index("tm")
    right, left = lax.rem(me + 2, count), lax.rem(me + count - 2, count)
    side = me + 1 - 2 * (me % 2)
    for peer in (right, left, side):
        signal(tm=peer)
    pl.semaphore_wait(pltpu.get_barrier_semaphore(), 3)
    size = mine_ref.shape[0] // 2
    chunks = [pl.ds(chunk * size, size) for chunk in range(2)]
    left_side, right_side = (peer + 1 - 2 * (peer % 2) for peer in (left, right))

    def give(index, owner, chunk, peer, src=None):
        dst = all_ref.at[owner, chunks[chunk]]
        return send(dst if src is None else src.at[chunks[chunk]], dst, ring_sems, index, tm=peer)

    to_side, to_right, to_left = [], [], []
    for chunk in range(2):
        to_side.append(give(chunk, me, chunk, side, mine_ref))
        to_right.append(give(2 + chunk, me, chunk, right, mine_ref))
        to_left.append(give(4 + chunk, me, chunk, left, mine_ref))
    own = pltpu.make_async_copy(mine_ref, all_ref.at[me], own_sem)
    own.start()
    onward, far = [], []
    for chunk in range(2):
        to_side[chunk].wait_recv()
        onward.append(give(6 + chunk, side, chunk, right))
        onward.append(give(8 + chunk, side, chunk, left))
        if chunk == 0:
            to_right[0].wait_recv()
            far.append(give(10, left, 0, right))
        else:
            to_left[1].wait_recv()
            far.append(give(11, right, 1, left))
    onward[0].wait_recv()
    far.append(give(12, left_side, 0, right))
    onward[3].wait_recv()
    far.append(give(13, right_side, 1, left))
    for copy in (to_right[1], to_left[0], onward[1], onward[2]):
        copy.wait_recv()
    for copy in to_side + to_right + to_left + onward:
        copy.wait_send()
    own.wait()
    for copy in far:
        copy.wait()


def gather(piece, count):
    size = piece.size * 2
    return pl.pallas_call(
        functools.partial(gather_kernel, count),
        out_shape=jax.ShapeDtypeStruct((count,) + piece.shape, piece.dtype),
        in_specs=[pl.BlockSpec(memory_space=pltpu.VMEM)],
        out_specs=pl.BlockSpec(memory_space=pl.ANY),
        scratch_shapes=[
            pltpu.SemaphoreType.DMA((14,)),
            pltpu.SemaphoreType.DMA((14,)),
            pltpu.SemaphoreType.DMA,
        ],
        compiler_params=pltpu.CompilerParams(
            collective_id=34, has_side_effects=True, skip_device_barrier=True
        ),
        cost_estimate=pl.CostEstimate(
            flops=0, transcendentals=0, bytes_accessed=32 * count * size
        ),
    )(piece)


def whiten_kernel(
    count, dead_ref, partner_ref, x_ref, first_ref, twiddle_ref, second_ref, *refs
):
    o_ref, *index_refs, flat, spec = refs
    for turn, index_ref in enumerate(index_refs):
        index_ref[0] = partner_ref[turn, 0] // 2
    blocks, width, samples = x_ref.shape
    step = flat.shape[0] // R1
    per = samples // SEG
    limit = count * width - dead_ref[0] - lax.axis_index("tm") * width
    for j in range(blocks):
        for q in range(per):
            start = (j * per + q) * step
            flat[start : start + width, :] = x_ref[j, :, q * SEG : (q + 1) * SEG].astype(
                jnp.float32
            )
    cos, sin = twiddle_ref[0], twiddle_ref[1]
    turned = []
    for c in range(width):
        series = flat[pl.ds(c, R1, stride=step), :].astype(jnp.bfloat16)
        part = jnp.dot(first_ref[...], series, preferred_element_type=jnp.float32)
        real = part[:R1] + part[2 * R1 : 3 * R1]
        imag = part[R1 : 2 * R1] + part[3 * R1 :]
        turned.append(
            jnp.concatenate([real * cos + imag * sin, imag * cos - real * sin], axis=1)
        )
    turned = jnp.concatenate(turned, axis=0)
    high = turned.astype(jnp.bfloat16)
    low = (turned - high.astype(jnp.float32)).astype(jnp.bfloat16)
    both = jnp.dot(high, second_ref[...], preferred_element_type=jnp.float32)
    result = jnp.dot(low, second_ref[:, : 2 * R2], preferred_element_type=jnp.float32)
    result = result + both[:, 2 * R2 :] + both[:, : 2 * R2]
    for c in range(width):
        spec[pl.ds(c, R1, stride=step), :] = result[c * R1 : (c + 1) * R1]
    lane = lax.broadcasted_iota(jnp.int32, (width, 2 * R2), 1) % R2
    channel = lax.broadcasted_iota(jnp.int32, (width, 2 * R2), 0)
    alive = (channel < limit).astype(jnp.float32)
    power = []
    for kappa in range(R1):
        square = jnp.square(spec[kappa * step : kappa * step + width, :])
        power.append(square + pltpu.roll(square, R2, 1))
    upto, total = [], None
    for kappa in range(R1):
        total = power[kappa] if total is None else total + power[kappa]
        upto.append(total)
    rest = None
    for kappa in reversed(range(R1)):
        rest = power[kappa] if rest is None else rest + power[kappa]
        below = jnp.where(lane == 0, 0.0, pltpu.roll(rest, 1, 1))
        above = jnp.where(lane == R2 - 1, 0.0, pltpu.roll(upto[kappa], 2 * R2 - 1, 1))
        smooth = (below + total + above) * (1.0 / (2 * WH + 1))
        factor = alive * lax.rsqrt(smooth + epsilon)
        piece = spec[kappa * step : kappa * step + width, :] * factor
        o_ref[kappa] = piece.astype(jnp.bfloat16)


def whiten(dead_counts, partner, x):
    first, twiddle, second = forward_constants()
    count, width, _ = x.shape
    rounds = partner.shape[0]
    rows = R1 * (width + 8)
    vmem = pl.BlockSpec(memory_space=pltpu.VMEM)
    smem = pl.BlockSpec(memory_space=pltpu.SMEM)
    return pl.pallas_call(
        functools.partial(whiten_kernel, count),
        out_shape=(jax.ShapeDtypeStruct((R1, width, 2 * R2), jnp.bfloat16),)
        + (jax.ShapeDtypeStruct((1,), jnp.int32),) * rounds,
        in_specs=[smem] * 2 + [vmem] * 4,
        out_specs=(vmem,) + (smem,) * rounds,
        scratch_shapes=[
            pltpu.VMEM((rows, SEG), jnp.float32),
            pltpu.VMEM((rows, 2 * R2), jnp.float32),
        ],
    )(
        dead_counts,
        partner,
        x,
        jnp.asarray(first, jnp.bfloat16),
        jnp.asarray(twiddle, jnp.float32),
        jnp.asarray(second, jnp.bfloat16),
    )


def quarter_turn(panel):
    lanes = panel.shape[1]
    wide = pltpu.roll(panel.astype(jnp.float32), lanes // 2, 1)
    left = lax.broadcasted_iota(jnp.int32, panel.shape, 1) < lanes // 2
    return jnp.where(left, wide, -wide).astype(jnp.bfloat16)


def times(table, panel):
    return lax.dot_general(
        table, panel, (((1,), (1,)), ((), ())), preferred_element_type=jnp.float32
    )


def stacked(rows):
    return jnp.concatenate([jnp.concatenate(row, axis=1) for row in rows], axis=0)


def transforms(table_ref, panel, signs, keep):
    def product(index, first, second):
        plain, turned = (first, second), (quarter_turn(first), quarter_turn(second))
        rows = {0: list(plain), 1: [turned[0], -turned[1]], -1: [-turned[0], turned[1]]}
        return times(table_ref[index], stacked([rows[sign] for sign in signs]))

    first, second = panel(0), panel(HALF)
    keep(0, product(0, first, second) + product(HALF, second, first))

    def step(p, carry):
        keep(p, product(p, panel(p), panel(R1 - p)))
        return carry

    lax.fori_loop(1, HALF, step, 0)


def transform_own(table_ref, own_ref, aa):
    parts, _, width, lanes = own_ref.shape
    channels = parts * width
    step = aa.shape[0] // (2 * R1)

    def keep(p, part):
        for h in range(2):
            for e in range(2):
                start = pl.multiple_of((2 * HALF * e + HALF * h + p) * step, 8)
                aa[pl.ds(start, SEG), :] = part[
                    h * SEG : (h + 1) * SEG, e * channels : (e + 1) * channels
                ]

    transforms(table_ref, lambda k: own_ref[:, k].reshape(channels, lanes), (0, 1), keep)


def multiply_round(table_ref, their_ref, aa, bb, ss):
    width = their_ref.shape[1]
    step = aa.shape[0] // (2 * R1)
    gap = ss.shape[0] // (2 * SEG)
    odd = lax.broadcasted_iota(jnp.int32, (SEG, 4 * width), 1) // width % 2 == 1

    def keep(p, part):
        for h in range(2):
            start = pl.multiple_of((HALF * h + p) * step, 8)
            kept = part[h * SEG : (h + 1) * SEG]
            bb[pl.ds(start, SEG), :] = jnp.where(odd, -kept, kept) if h else kept

    transforms(table_ref, lambda k: their_ref[k], (0, -1, 1, 0), keep)

    def multiply(f, carry):
        mine = aa[pl.ds(f, 2 * R1, stride=step), :].astype(jnp.bfloat16)
        their = bb[pl.ds(f, R1, stride=step), :]
        their = jnp.concatenate([their[:, : 2 * width], their[:, 2 * width :]], axis=0)
        product = lax.dot_general(
            their.astype(jnp.bfloat16),
            mine,
            (((0,), (0,)), ((), ())),
            preferred_element_type=jnp.float32,
        )
        for part in range(2):
            start = pl.multiple_of((2 * f + part) * gap, 8)
            ss[pl.ds(start, width), :] = product[part * width : (part + 1) * width]
        return carry

    lax.fori_loop(0, SEG, multiply, 0, unroll=8)


def head_kernel(own_ref, their_ref, ta_ref, tb_ref, aa, ss, bb):
    transform_own(ta_ref, own_ref, aa)
    multiply_round(tb_ref, their_ref, aa, bb, ss)


def tail_kernel(aa, head_ref, their_ref, tb_ref, lag_ref, o_ref, ss, bb):
    multiply_round(tb_ref, their_ref, aa, bb, ss)
    width, channels = their_ref.shape[1], aa.shape[1]
    gap = ss.shape[0] // (2 * SEG)
    for b in range(width):
        pieces = [
            ref[pl.ds(b, 2 * SEG, stride=gap), :].astype(jnp.bfloat16) for ref in (head_ref, ss)
        ]
        start = 2 * b * channels
        o_ref[:, start : start + 2 * channels] = jnp.dot(
            lag_ref[...], jnp.concatenate(pieces, axis=1), preferred_element_type=jnp.float32
        )


VMEM_LIMIT = 28 * 2**20


def product_shape(width, channels):
    return 2 * SEG * (width + 8), channels


def head(tables, own, their):
    parts, _, width, _ = own.shape
    channels = parts * width
    vmem = pl.BlockSpec(memory_space=pltpu.VMEM)
    return pl.pallas_call(
        head_kernel,
        out_shape=(
            jax.ShapeDtypeStruct((2 * R1 * (SEG + 8), channels), jnp.float32),
            jax.ShapeDtypeStruct(product_shape(width, channels), jnp.float32),
        ),
        in_specs=[vmem] * 4,
        out_specs=(vmem, vmem),
        scratch_shapes=[pltpu.VMEM((R1 * (SEG + 8), 4 * width), jnp.float32)],
        compiler_params=pltpu.CompilerParams(vmem_limit_bytes=VMEM_LIMIT),
        cost_estimate=pl.CostEstimate(
            flops=2 * 10**9, transcendentals=0, bytes_accessed=32 * 2**20
        ),
    )(own, their, *tables)


def tail(table, panel, product, their):
    width, channels = their.shape[1], panel.shape[1]
    vmem = pl.BlockSpec(memory_space=pltpu.VMEM)
    return pl.pallas_call(
        tail_kernel,
        out_shape=jax.ShapeDtypeStruct((LAGS, width * 2 * channels), jnp.float32),
        in_specs=[vmem] * 5,
        out_specs=vmem,
        scratch_shapes=[
            pltpu.VMEM(product_shape(width, channels), jnp.float32),
            pltpu.VMEM((R1 * (SEG + 8), 4 * width), jnp.float32),
        ],
        compiler_params=pltpu.CompilerParams(vmem_limit_bytes=VMEM_LIMIT),
    )(panel, product, their, table, jnp.asarray(lag_table(), jnp.bfloat16))


def permuted(bits, count, piece):
    if not bits:
        return piece
    return lax.ppermute(piece, "chan", [(i, i ^ bits) for i in range(count)])


def per_device(strain, dead_counts, partner):
    channels = strain.shape[0]
    count, blocks = lax.axis_size("tm"), lax.axis_size("chan")
    width = channels // count
    piece, *indices = whiten(dead_counts, partner, scatter(strain, count, width))
    sent = pick_core(partner, piece)
    tables = [
        jnp.asarray(segment_table(low, high), jnp.bfloat16)
        for low, high in ((-LAGS // 2, SEG + LAGS // 2), (0, SEG))
    ]

    def first(bits):
        def branch(mine, held):
            return permuted(bits, blocks, held), gather(mine, count)

        return branch

    def second(bits):
        def branch(held, own, their, *tables):
            return permuted(bits, blocks, held), head(tables, own, their)

        return branch

    masks = range(0, blocks, 2)
    their, own = lax.switch(indices[0][0], [first(bits) for bits in masks], piece, sent[0])
    other, (panel, product) = lax.switch(
        indices[1][0], [second(bits) for bits in masks], sent[1], own, their, *tables
    )
    return tail(tables[1], panel, product, other)


def solution(mesh):
    return jax.shard_map(
        per_device,
        mesh=mesh,
        in_specs=(P("chan", "tm"), P("chan"), P()),
        out_specs=P(None, ("chan", "tm")),
        check_vma=False,
    )
```

```python
import functools
import math

import jax
import jax.numpy as jnp
import numpy as np
from jax import lax
from jax.experimental import pallas as pl
from jax.experimental.pallas import tpu as pltpu
from jax.sharding import PartitionSpec as P

NF = 2048
WH = 32
LAGS = 128
NT = 4096
epsilon = 1e-05

R1 = 32
R2 = NF // R1
SEG = NT // R1
HALF = R1 // 2


def split_bf16(table):
    table = np.asarray(table, np.float32)
    high = table.astype(np.dtype(jnp.bfloat16)).astype(np.float32)
    return high, table - high


@functools.cache
def forward_constants():
    kappa, t1 = np.arange(R1), np.arange(R1)
    phase = 2 * np.pi * (kappa[:, None] * t1[None, :] % R1) / R1
    first = np.concatenate([np.cos(phase), -np.sin(phase)], axis=0)
    first = np.concatenate(split_bf16(first), axis=0)
    t0 = np.arange(SEG)
    phase = 2 * np.pi * (kappa[:, None] * t0[None, :]) / NT
    amplitude = 1 / math.sqrt(NT)
    twiddle = np.stack([np.cos(phase) * amplitude, np.sin(phase) * amplitude])
    k2 = np.arange(R2)
    phase = 2 * np.pi * (t0[:, None] * k2[None, :] % SEG) / SEG
    cos, sin = np.cos(phase), np.sin(phase)
    second = np.block([[cos, -sin], [sin, cos]])
    second = np.concatenate(split_bf16(second), axis=1)
    return first.astype(np.float32), twiddle.astype(np.float32), second.astype(np.float32)


def window_sums(low, high):
    x = np.arange(-2 * NT, 2 * NT)
    u = np.arange(low, high)
    return np.exp(2j * np.pi * (x[:, None] * u[None, :] % NT) / NT).sum(1)


@functools.cache
def segment_table(low, high):
    sums = window_sums(low, high)
    f, k2 = np.arange(SEG), np.arange(R2)
    out = np.zeros((HALF + 1, 2, SEG, 2, 2, R2))
    for p in range(HALF + 1):
        classes = (p % HALF, R1 - p if p % HALF else HALF)
        for h, target in enumerate(classes):
            for g in range(2):
                if p % HALF:
                    source, mirrored = classes[g], g != h
                elif g == h and p == 0:
                    source, mirrored = target, False
                elif g != h and p == HALF:
                    source, mirrored = target, True
                else:
                    continue
                k = (-1 if mirrored else 1) * (source + R1 * k2)
                part = sums[k[None, :] - R1 // 2 * f[:, None] - R1 // 4 + 2 * NT]
                if source == 0:
                    part[:, 0] *= 0.0 if mirrored else math.sqrt(2.0)
                out[p, h, :, g, 0] = part.real
                out[p, h, :, g, 1] = part.imag if mirrored else -part.imag
    return out.reshape(HALF + 1, 2 * SEG, 4 * R2).astype(np.float32)


@functools.cache
def lag_table():
    tau, f = np.arange(LAGS) - LAGS // 2, np.arange(SEG)
    phase = 2 * np.pi * (f[None, :] + 0.5) * tau[:, None] / (2 * SEG)
    table = np.stack([np.cos(phase), -np.sin(phase)], axis=-1)
    scale = 1 / (2.0**19 * math.sqrt(2.0))
    return (table * scale).reshape(LAGS, 2 * SEG).astype(np.float32)


MESH = pl.DeviceIdType.MESH


def signal(**target):
    barrier = pltpu.get_barrier_semaphore()
    pl.semaphore_signal(barrier, inc=1, device_id=target, device_id_type=MESH)


def send(src, dst, sems, index, **target):
    copy = pltpu.make_async_remote_copy(
        src_ref=src,
        dst_ref=dst,
        send_sem=sems[0].at[index],
        recv_sem=sems[1].at[index],
        device_id=target,
        device_id_type=MESH,
    )
    copy.start()
    return copy


def scatter_kernel(count, width, x_ref, o_ref, send_sem, recv_sem, own_sem):
    me = lax.axis_index("tm")
    peers = [lax.rem(me + step, count) for step in range(1, count)]
    for peer in peers:
        signal(tm=peer)
    pl.semaphore_wait(pltpu.get_barrier_semaphore(), len(peers))

    def rows(index):
        return x_ref.at[pl.ds(pl.multiple_of(index * width, width), width), :]

    copies = [
        send(rows(peer), o_ref.at[me], (send_sem, recv_sem), step, tm=peer)
        for step, peer in enumerate(peers)
    ]
    own = pltpu.make_async_copy(rows(me), o_ref.at[me], own_sem)
    own.start()
    own.wait()
    for copy in copies:
        copy.wait()


def scatter(strain, count, width):
    return pl.pallas_call(
        functools.partial(scatter_kernel, count, width),
        out_shape=jax.ShapeDtypeStruct((count, width, strain.shape[1]), strain.dtype),
        in_specs=[pl.BlockSpec(memory_space=pltpu.VMEM)],
        out_specs=pl.BlockSpec(memory_space=pl.ANY),
        scratch_shapes=[
            pltpu.SemaphoreType.DMA((count,)),
            pltpu.SemaphoreType.DMA((count,)),
            pltpu.SemaphoreType.DMA,
        ],
        compiler_params=pltpu.CompilerParams(
            collective_id=32, has_side_effects=True, skip_device_barrier=True
        ),
    )(strain)


def beside_kernel(rounds, partner_ref, x_ref, *refs):
    out_refs, got, send_sem, recv_sem = refs[:rounds], *refs[rounds:]
    block = lax.axis_index("chan")
    beside = block + 1 - 2 * (block % 2)
    signal(chan=beside)
    pl.semaphore_wait(pltpu.get_barrier_semaphore(), 1)
    copy = send(x_ref, got, (send_sem, recv_sem), 0, chan=beside)
    copy.wait()
    for turn, out_ref in enumerate(out_refs):
        out_ref[...] = jnp.where(partner_ref[turn, 0] % 2 == 1, got[...], x_ref[...])


def pick_core(partner, piece):
    rounds = partner.shape[0]
    vmem = pl.BlockSpec(memory_space=pltpu.VMEM)
    return pl.pallas_call(
        functools.partial(beside_kernel, rounds),
        out_shape=(jax.ShapeDtypeStruct(piece.shape, piece.dtype),) * rounds,
        in_specs=[pl.BlockSpec(memory_space=pltpu.SMEM), vmem],
        out_specs=(vmem,) * rounds,
        scratch_shapes=[
            pltpu.VMEM(piece.shape, piece.dtype),
            pltpu.SemaphoreType.DMA((1,)),
            pltpu.SemaphoreType.DMA((1,)),
        ],
        compiler_params=pltpu.CompilerParams(
            collective_id=33, has_side_effects=True, skip_device_barrier=True
        ),
    )(partner, piece)


def gather_kernel(count, half, mine_ref, all_ref, *sems):
    ring_sems, own_sem = sems[:2], sems[2]
    me = lax.axis_index("tm")
    right, left = lax.rem(me + 2, count), lax.rem(me + count - 2, count)
    side = me + 1 - 2 * (me % 2)
    for peer in (right, left, side):
        signal(tm=peer)
    pl.semaphore_wait(pltpu.get_barrier_semaphore(), 3)
    mine_ref = mine_ref.at[pl.ds(half * HALF, HALF)]
    size = HALF // 2
    chunks = [pl.ds(chunk * size, size) for chunk in range(2)]
    left_side, right_side = (peer + 1 - 2 * (peer % 2) for peer in (left, right))

    def give(index, owner, chunk, peer, src=None):
        dst = all_ref.at[owner, chunks[chunk]]
        return send(dst if src is None else src.at[chunks[chunk]], dst, ring_sems, index, tm=peer)

    to_side, to_right, to_left = [], [], []
    for chunk in range(2):
        to_side.append(give(chunk, me, chunk, side, mine_ref))
        to_right.append(give(2 + chunk, me, chunk, right, mine_ref))
        to_left.append(give(4 + chunk, me, chunk, left, mine_ref))
    own = pltpu.make_async_copy(mine_ref, all_ref.at[me], own_sem)
    own.start()
    onward, far = [], []
    for chunk in range(2):
        to_side[chunk].wait_recv()
        onward.append(give(6 + chunk, side, chunk, right))
        onward.append(give(8 + chunk, side, chunk, left))
        if chunk == 0:
            to_right[0].wait_recv()
            far.append(give(10, left, 0, right))
        else:
            to_left[1].wait_recv()
            far.append(give(11, right, 1, left))
    onward[0].wait_recv()
    far.append(give(12, left_side, 0, right))
    onward[3].wait_recv()
    far.append(give(13, right_side, 1, left))
    for copy in (to_right[1], to_left[0], onward[1], onward[2]):
        copy.wait_recv()
    for copy in to_side + to_right + to_left + onward:
        copy.wait_send()
    own.wait()
    for copy in far:
        copy.wait()


def gather(piece, count, half):
    shape = (count, HALF) + piece.shape[1:]
    return pl.pallas_call(
        functools.partial(gather_kernel, count, half),
        out_shape=jax.ShapeDtypeStruct(shape, piece.dtype),
        in_specs=[pl.BlockSpec(memory_space=pltpu.VMEM)],
        out_specs=pl.BlockSpec(memory_space=pl.ANY),
        scratch_shapes=[
            pltpu.SemaphoreType.DMA((14,)),
            pltpu.SemaphoreType.DMA((14,)),
            pltpu.SemaphoreType.DMA,
        ],
        compiler_params=pltpu.CompilerParams(
            collective_id=34 + half, has_side_effects=True, skip_device_barrier=True
        ),
        cost_estimate=pl.CostEstimate(
            flops=0, transcendentals=0, bytes_accessed=32 * math.prod(shape)
        ),
    )(piece)


def whiten_kernel(
    count, dead_ref, partner_ref, x_ref, first_ref, twiddle_ref, second_ref, *refs
):
    o_ref, *index_refs, flat, spec = refs
    for turn, index_ref in enumerate(index_refs):
        index_ref[0] = partner_ref[turn, 0] // 2
    blocks, width, samples = x_ref.shape
    step = flat.shape[0] // R1
    per = samples // SEG
    limit = count * width - dead_ref[0] - lax.axis_index("tm") * width
    for j in range(blocks):
        for q in range(per):
            start = (j * per + q) * step
            flat[start : start + width, :] = x_ref[j, :, q * SEG : (q + 1) * SEG].astype(
                jnp.float32
            )
    cos, sin = twiddle_ref[0], twiddle_ref[1]
    turned = []
    for c in range(width):
        series = flat[pl.ds(c, R1, stride=step), :].astype(jnp.bfloat16)
        part = jnp.dot(first_ref[...], series, preferred_element_type=jnp.float32)
        real = part[:R1] + part[2 * R1 : 3 * R1]
        imag = part[R1 : 2 * R1] + part[3 * R1 :]
        turned.append(
            jnp.concatenate([real * cos + imag * sin, imag * cos - real * sin], axis=1)
        )
    turned = jnp.concatenate(turned, axis=0)
    high = turned.astype(jnp.bfloat16)
    low = (turned - high.astype(jnp.float32)).astype(jnp.bfloat16)
    both = jnp.dot(high, second_ref[...], preferred_element_type=jnp.float32)
    result = jnp.dot(low, second_ref[:, : 2 * R2], preferred_element_type=jnp.float32)
    result = result + both[:, 2 * R2 :] + both[:, : 2 * R2]
    for c in range(width):
        spec[pl.ds(c, R1, stride=step), :] = result[c * R1 : (c + 1) * R1]
    lane = lax.broadcasted_iota(jnp.int32, (width, 2 * R2), 1) % R2
    channel = lax.broadcasted_iota(jnp.int32, (width, 2 * R2), 0)
    alive = (channel < limit).astype(jnp.float32)
    power = []
    for kappa in range(R1):
        square = jnp.square(spec[kappa * step : kappa * step + width, :])
        power.append(square + pltpu.roll(square, R2, 1))
    upto, total = [], None
    for kappa in range(R1):
        total = power[kappa] if total is None else total + power[kappa]
        upto.append(total)
    rest = None
    for kappa in reversed(range(R1)):
        rest = power[kappa] if rest is None else rest + power[kappa]
        below = jnp.where(lane == 0, 0.0, pltpu.roll(rest, 1, 1))
        above = jnp.where(lane == R2 - 1, 0.0, pltpu.roll(upto[kappa], 2 * R2 - 1, 1))
        smooth = (below + total + above) * (1.0 / (2 * WH + 1))
        factor = alive * lax.rsqrt(smooth + epsilon)
        piece = spec[kappa * step : kappa * step + width, :] * factor
        o_ref[kappa] = piece.astype(jnp.bfloat16)


def whiten(dead_counts, partner, x):
    first, twiddle, second = forward_constants()
    count, width, _ = x.shape
    rounds = partner.shape[0]
    rows = R1 * (width + 8)
    vmem = pl.BlockSpec(memory_space=pltpu.VMEM)
    smem = pl.BlockSpec(memory_space=pltpu.SMEM)
    return pl.pallas_call(
        functools.partial(whiten_kernel, count),
        out_shape=(jax.ShapeDtypeStruct((R1, width, 2 * R2), jnp.bfloat16),)
        + (jax.ShapeDtypeStruct((1,), jnp.int32),) * rounds,
        in_specs=[smem] * 2 + [vmem] * 4,
        out_specs=(vmem,) + (smem,) * rounds,
        scratch_shapes=[
            pltpu.VMEM((rows, SEG), jnp.float32),
            pltpu.VMEM((rows, 2 * R2), jnp.float32),
        ],
    )(
        dead_counts,
        partner,
        x,
        jnp.asarray(first, jnp.bfloat16),
        jnp.asarray(twiddle, jnp.float32),
        jnp.asarray(second, jnp.bfloat16),
    )


def quarter_turn(panel):
    lanes = panel.shape[1]
    wide = pltpu.roll(panel.astype(jnp.float32), lanes // 2, 1)
    left = lax.broadcasted_iota(jnp.int32, panel.shape, 1) < lanes // 2
    return jnp.where(left, wide, -wide).astype(jnp.bfloat16)


def correlate_kernel(low_ref, high_ref, *refs):
    rounds = len(refs) - 7
    their_refs = refs[:rounds]
    ta_ref, tb_ref, lag_ref, o_ref, aa, bb, ss = refs[rounds:]
    parts, _, width, lanes = low_ref.shape
    channels = parts * width
    pairs = rounds * width
    step = aa.shape[0] // (2 * R1)

    def times(table, panel):
        return lax.dot_general(
            table, panel, (((1,), (1,)), ((), ())), preferred_element_type=jnp.float32
        )

    def panels(p, q):
        mine = [low_ref[:, p].reshape(channels, lanes), high_ref[:, q].reshape(channels, lanes)]
        their = [
            jnp.concatenate([ref[k] for ref in their_refs], axis=0) for k in (p, HALF + q)
        ]
        return [(side, quarter_turn(side)) for side in mine + their]

    def products(index, mine, their):
        (one, turned_one), (two, turned_two) = mine
        rows = [[one, two], [turned_one, -turned_two]]
        part = times(
            ta_ref[index], jnp.concatenate([jnp.concatenate(r, axis=1) for r in rows], axis=0)
        )
        (one, turned_one), (two, turned_two) = their
        rows = [[one, two], [-turned_one, turned_two], [turned_one, -turned_two], [one, two]]
        other = times(
            tb_ref[index], jnp.concatenate([jnp.concatenate(r, axis=1) for r in rows], axis=0)
        )
        return part, other

    group = lax.broadcasted_iota(jnp.int32, (SEG, 4 * pairs), 1) // pairs
    odd = group % 2 == 1

    def keep(p, part, other):
        for h in range(2):
            rows = slice(h * SEG, (h + 1) * SEG)
            for e in range(2):
                start = pl.multiple_of((2 * HALF * e + HALF * h + p) * step, 8)
                aa[pl.ds(start, SEG), :] = part[rows, e * channels : (e + 1) * channels]
            start = pl.multiple_of((HALF * h + p) * step, 8)
            kept = other[rows]
            bb[pl.ds(start, SEG), :] = jnp.where(odd, -kept, kept) if h else kept

    ends = panels(0, 0)
    part, other = products(0, ends[:2], ends[2:])
    mirrored, mirrored_other = products(HALF, ends[1::-1], ends[:1:-1])
    keep(0, part + mirrored, other + mirrored_other)

    def transform(p, carry):
        sides = panels(p, HALF - p)
        keep(p, *products(p, sides[:2], sides[2:]))
        return carry

    lax.fori_loop(1, HALF, transform, 0, unroll=5)
    gap = ss.shape[0] // (2 * SEG)

    def multiply(f, carry):
        mine = aa[pl.ds(f, 2 * R1, stride=step), :].astype(jnp.bfloat16)
        their = bb[pl.ds(f, R1, stride=step), :]
        their = jnp.concatenate([their[:, : 2 * pairs], their[:, 2 * pairs :]], axis=0)
        product = lax.dot_general(
            their.astype(jnp.bfloat16),
            mine,
            (((0,), (0,)), ((), ())),
            preferred_element_type=jnp.float32,
        )
        for part in range(2):
            start = pl.multiple_of((2 * f + part) * gap, 8)
            ss[pl.ds(start, pairs), :] = product[part * pairs : (part + 1) * pairs]
        return carry

    lax.fori_loop(0, SEG, multiply, 0, unroll=8)

    for b in range(width):
        pieces = [
            ss[pl.ds(turn * width + b, 2 * SEG, stride=gap), :].astype(jnp.bfloat16)
            for turn in range(rounds)
        ]
        start = b * rounds * channels
        o_ref[:, start : start + rounds * channels] = jnp.dot(
            lag_ref[...], jnp.concatenate(pieces, axis=1), preferred_element_type=jnp.float32
        )


def correlate(low, high, theirs):
    parts, _, width, lanes = low.shape
    channels = parts * width
    rounds = len(theirs)
    vmem = pl.BlockSpec(memory_space=pltpu.VMEM)
    return pl.pallas_call(
        correlate_kernel,
        out_shape=jax.ShapeDtypeStruct((LAGS, width * rounds * channels), jnp.float32),
        in_specs=[vmem] * (rounds + 5),
        out_specs=vmem,
        scratch_shapes=[
            pltpu.VMEM((2 * R1 * (SEG + 8), channels), jnp.float32),
            pltpu.VMEM((R1 * (SEG + 8), 4 * rounds * width), jnp.float32),
            pltpu.VMEM((2 * SEG * (rounds * width + 8), channels), jnp.float32),
        ],
        compiler_params=pltpu.CompilerParams(vmem_limit_bytes=28 * 2**20),
    )(
        low,
        high,
        *theirs,
        jnp.asarray(segment_table(-LAGS // 2, SEG + LAGS // 2), jnp.bfloat16),
        jnp.asarray(segment_table(0, SEG), jnp.bfloat16),
        jnp.asarray(lag_table(), jnp.bfloat16),
    )


def permuted(bits, count, piece):
    if not bits:
        return piece
    return lax.ppermute(piece, "chan", [(i, i ^ bits) for i in range(count)])


def per_device(strain, dead_counts, partner):
    channels = strain.shape[0]
    count, blocks = lax.axis_size("tm"), lax.axis_size("chan")
    width = channels // count
    piece, *indices = whiten(dead_counts, partner, scatter(strain, count, width))
    sent = pick_core(partner, piece)

    def route(bits, half):
        def branch(mine, held):
            return permuted(bits, blocks, held), gather(mine, count, half)

        return branch

    theirs, own = [], []
    for turn, (index, held) in enumerate(zip(indices, sent)):
        routes = [route(bits, turn) for bits in range(0, blocks, 2)]
        their, part = lax.switch(index[0], routes, piece, held)
        theirs.append(their)
        own.append(part)
    return correlate(*own, theirs)


def solution(mesh):
    return jax.shard_map(
        per_device,
        mesh=mesh,
        in_specs=(P("chan", "tm"), P("chan"), P()),
        out_specs=P(None, ("chan", "tm")),
        check_vma=False,
    )
```

```python
import functools
import math

import jax
import jax.numpy as jnp
import numpy as np
from jax import lax
from jax.experimental import pallas as pl
from jax.experimental.pallas import tpu as pltpu
from jax.sharding import PartitionSpec as P

NF = 2048
WH = 32
LAGS = 128
NT = 4096
epsilon = 1e-05

R1 = 32
R2 = NF // R1
SEG = NT // R1
HALF = R1 // 2


def split_bf16(table):
    table = np.asarray(table, np.float32)
    high = table.astype(np.dtype(jnp.bfloat16)).astype(np.float32)
    return high, table - high


@functools.cache
def forward_constants():
    kappa, t1 = np.arange(R1), np.arange(R1)
    phase = 2 * np.pi * (kappa[:, None] * t1[None, :] % R1) / R1
    first = np.concatenate([np.cos(phase), -np.sin(phase)], axis=0)
    first = np.concatenate(split_bf16(first), axis=0)
    t0 = np.arange(SEG)
    phase = 2 * np.pi * (kappa[:, None] * t0[None, :]) / NT
    amplitude = 1 / math.sqrt(NT)
    twiddle = np.stack([np.cos(phase) * amplitude, np.sin(phase) * amplitude])
    k2 = np.arange(R2)
    phase = 2 * np.pi * (t0[:, None] * k2[None, :] % SEG) / SEG
    cos, sin = np.cos(phase), np.sin(phase)
    second = np.block([[cos, -sin], [sin, cos]])
    second = np.concatenate(split_bf16(second), axis=1)
    return first.astype(np.float32), twiddle.astype(np.float32), second.astype(np.float32)


def window_sums(low, high):
    x = np.arange(-2 * NT, 2 * NT)
    u = np.arange(low, high)
    return np.exp(2j * np.pi * (x[:, None] * u[None, :] % NT) / NT).sum(1)


@functools.cache
def segment_table(low, high):
    sums = window_sums(low, high)
    f, k2 = np.arange(SEG), np.arange(R2)
    out = np.zeros((HALF + 1, 2, SEG, 2, 2, R2))
    for p in range(HALF + 1):
        classes = (p % HALF, R1 - p if p % HALF else HALF)
        for h, target in enumerate(classes):
            for g in range(2):
                if p % HALF:
                    source, mirrored = classes[g], g != h
                elif g == h and p == 0:
                    source, mirrored = target, False
                elif g != h and p == HALF:
                    source, mirrored = target, True
                else:
                    continue
                k = (-1 if mirrored else 1) * (source + R1 * k2)
                part = sums[k[None, :] - R1 // 2 * f[:, None] - R1 // 4 + 2 * NT]
                if source == 0:
                    part[:, 0] *= 0.0 if mirrored else math.sqrt(2.0)
                out[p, h, :, g, 0] = part.real
                out[p, h, :, g, 1] = part.imag if mirrored else -part.imag
    return out.reshape(HALF + 1, 2 * SEG, 4 * R2).astype(np.float32)


@functools.cache
def lag_table():
    tau, f = np.arange(LAGS) - LAGS // 2, np.arange(SEG)
    phase = 2 * np.pi * (f[None, :] + 0.5) * tau[:, None] / (2 * SEG)
    table = np.stack([np.cos(phase), -np.sin(phase)], axis=-1)
    scale = 1 / (2.0**19 * math.sqrt(2.0))
    return (table * scale).reshape(LAGS, 2 * SEG).astype(np.float32)


MESH = pl.DeviceIdType.MESH


def signal(**target):
    barrier = pltpu.get_barrier_semaphore()
    pl.semaphore_signal(barrier, inc=1, device_id=target, device_id_type=MESH)


def send(src, dst, sems, index, **target):
    copy = pltpu.make_async_remote_copy(
        src_ref=src,
        dst_ref=dst,
        send_sem=sems[0].at[index],
        recv_sem=sems[1].at[index],
        device_id=target,
        device_id_type=MESH,
    )
    copy.start()
    return copy


def scatter_kernel(count, width, x_ref, o_ref, send_sem, recv_sem, own_sem):
    me = lax.axis_index("tm")
    peers = [lax.rem(me + step, count) for step in range(1, count)]
    for peer in peers:
        signal(tm=peer)
    pl.semaphore_wait(pltpu.get_barrier_semaphore(), len(peers))

    def rows(index):
        return x_ref.at[pl.ds(pl.multiple_of(index * width, width), width), :]

    copies = [
        send(rows(peer), o_ref.at[me], (send_sem, recv_sem), step, tm=peer)
        for step, peer in enumerate(peers)
    ]
    own = pltpu.make_async_copy(rows(me), o_ref.at[me], own_sem)
    own.start()
    own.wait()
    for copy in copies:
        copy.wait()


def scatter(strain, count, width):
    return pl.pallas_call(
        functools.partial(scatter_kernel, count, width),
        out_shape=jax.ShapeDtypeStruct((count, width, strain.shape[1]), strain.dtype),
        in_specs=[pl.BlockSpec(memory_space=pltpu.VMEM)],
        out_specs=pl.BlockSpec(memory_space=pl.ANY),
        scratch_shapes=[
            pltpu.SemaphoreType.DMA((count,)),
            pltpu.SemaphoreType.DMA((count,)),
            pltpu.SemaphoreType.DMA,
        ],
        compiler_params=pltpu.CompilerParams(
            collective_id=32, has_side_effects=True, skip_device_barrier=True
        ),
    )(strain)


def swap_kernel(bits, count, low_ref, high_ref, mine_ref, their_ref, all_ref, *sems):
    pair_sems, over_sems, ring_sems, own_sem = sems[0:2], sems[2:4], sems[4:6], sems[6]
    me, block = lax.axis_index("tm"), lax.axis_index("chan")
    right, left = lax.rem(me + 2, count), lax.rem(me + count - 2, count)
    side = me + 1 - 2 * (me % 2)
    partner = block
    for digit in range(bits.bit_length()):
        if bits >> digit & 1:
            partner = partner + 2**digit * (1 - 2 * (block // 2**digit % 2))
    beside = block + 1 - 2 * (block % 2)
    for peer in (right, left, side):
        signal(tm=peer)
    signal(chan=beside)
    if bits:
        signal(chan=partner)
    pl.semaphore_wait(pltpu.get_barrier_semaphore(), 4 + (bits > 0))
    size = mine_ref.shape[0] // 2
    chunks = [pl.ds(chunk * size, size) for chunk in range(2)]
    left_side, right_side = (peer + 1 - 2 * (peer % 2) for peer in (left, right))

    def give(index, owner, chunk, peer, src=None):
        dst = all_ref.at[owner, chunks[chunk]]
        return send(dst if src is None else src.at[chunks[chunk]], dst, ring_sems, index, tm=peer)

    to_side, to_right, to_left = [], [], []
    for chunk in range(2):
        to_side.append(give(chunk, me, chunk, side, mine_ref))
        to_right.append(give(2 + chunk, me, chunk, right, mine_ref))
        to_left.append(give(4 + chunk, me, chunk, left, mine_ref))
    halves = (low_ref, high_ref)
    if bits:
        pair = [
            send(half, their_ref.at[0, h], pair_sems, h, chan=partner)
            for h, half in enumerate(halves)
        ]
    else:
        pair = [
            pltpu.make_async_copy(half, their_ref.at[0, h], pair_sems[0].at[h])
            for h, half in enumerate(halves)
        ]
        for copy in pair:
            copy.start()
    own = pltpu.make_async_copy(mine_ref, all_ref.at[me], own_sem)
    own.start()
    onward, far = [], []
    for chunk in range(2):
        to_side[chunk].wait_recv()
        onward.append(give(6 + chunk, side, chunk, right))
        onward.append(give(8 + chunk, side, chunk, left))
        if chunk == 0:
            to_right[0].wait_recv()
            far.append(give(10, left, 0, right))
        else:
            to_left[1].wait_recv()
            far.append(give(11, right, 1, left))
    onward[0].wait_recv()
    far.append(give(12, left_side, 0, right))
    onward[3].wait_recv()
    far.append(give(13, right_side, 1, left))
    over = []
    for h, copy in enumerate(pair):
        if bits:
            copy.wait_recv()
        else:
            copy.wait()
        over.append(send(their_ref.at[0, h], their_ref.at[1, h], over_sems, h, chan=beside))
    for copy in (to_right[1], to_left[0], onward[1], onward[2]):
        copy.wait_recv()
    for copy in to_side + to_right + to_left + onward:
        copy.wait_send()
    if bits:
        for copy in pair:
            copy.wait_send()
    own.wait()
    for copy in far + over:
        copy.wait()


def swap(bits, count, low, high, mine):
    here = pl.BlockSpec(memory_space=pltpu.VMEM)
    there = pl.BlockSpec(memory_space=pl.ANY)
    return pl.pallas_call(
        functools.partial(swap_kernel, bits, count),
        out_shape=(
            jax.ShapeDtypeStruct((2, 2) + low.shape, low.dtype),
            jax.ShapeDtypeStruct((count,) + low.shape, low.dtype),
        ),
        in_specs=[here] * 3,
        out_specs=(there, there),
        scratch_shapes=[
            pltpu.SemaphoreType.DMA((2,)),
            pltpu.SemaphoreType.DMA((2,)),
            pltpu.SemaphoreType.DMA((2,)),
            pltpu.SemaphoreType.DMA((2,)),
            pltpu.SemaphoreType.DMA((14,)),
            pltpu.SemaphoreType.DMA((14,)),
            pltpu.SemaphoreType.DMA,
        ],
        compiler_params=pltpu.CompilerParams(
            collective_id=bits // 2, has_side_effects=True, skip_device_barrier=True
        ),
    )(low, high, mine)


def whiten_kernel(
    count, dead_ref, partner_ref, x_ref, first_ref, twiddle_ref, second_ref, *refs
):
    low_ref, high_ref, *index_refs, flat, spec = refs
    for turn, index_ref in enumerate(index_refs):
        index_ref[0] = partner_ref[turn, 0] // 2
    blocks, width, samples = x_ref.shape
    step = flat.shape[0] // R1
    per = samples // SEG
    limit = count * width - dead_ref[0] - lax.axis_index("tm") * width
    for j in range(blocks):
        for q in range(per):
            start = (j * per + q) * step
            flat[start : start + width, :] = x_ref[j, :, q * SEG : (q + 1) * SEG].astype(
                jnp.float32
            )
    cos, sin = twiddle_ref[0], twiddle_ref[1]
    turned = []
    for c in range(width):
        series = flat[pl.ds(c, R1, stride=step), :].astype(jnp.bfloat16)
        part = jnp.dot(first_ref[...], series, preferred_element_type=jnp.float32)
        real = part[:R1] + part[2 * R1 : 3 * R1]
        imag = part[R1 : 2 * R1] + part[3 * R1 :]
        turned.append(
            jnp.concatenate([real * cos + imag * sin, imag * cos - real * sin], axis=1)
        )
    turned = jnp.concatenate(turned, axis=0)
    high = turned.astype(jnp.bfloat16)
    low = (turned - high.astype(jnp.float32)).astype(jnp.bfloat16)
    both = jnp.dot(high, second_ref[...], preferred_element_type=jnp.float32)
    result = jnp.dot(low, second_ref[:, : 2 * R2], preferred_element_type=jnp.float32)
    result = result + both[:, 2 * R2 :] + both[:, : 2 * R2]
    for c in range(width):
        spec[pl.ds(c, R1, stride=step), :] = result[c * R1 : (c + 1) * R1]
    lane = lax.broadcasted_iota(jnp.int32, (width, 2 * R2), 1) % R2
    channel = lax.broadcasted_iota(jnp.int32, (width, 2 * R2), 0)
    alive = (channel < limit).astype(jnp.float32)
    power = []
    for kappa in range(R1):
        square = jnp.square(spec[kappa * step : kappa * step + width, :])
        power.append(square + pltpu.roll(square, R2, 1))
    upto, total = [], None
    for kappa in range(R1):
        total = power[kappa] if total is None else total + power[kappa]
        upto.append(total)
    rest = None
    for kappa in reversed(range(R1)):
        rest = power[kappa] if rest is None else rest + power[kappa]
        below = jnp.where(lane == 0, 0.0, pltpu.roll(rest, 1, 1))
        above = jnp.where(lane == R2 - 1, 0.0, pltpu.roll(upto[kappa], 2 * R2 - 1, 1))
        smooth = (below + total + above) * (1.0 / (2 * WH + 1))
        factor = alive * lax.rsqrt(smooth + epsilon)
        piece = spec[kappa * step : kappa * step + width, :] * factor
        half_ref = (low_ref, high_ref)[kappa // HALF]
        half_ref[kappa % HALF] = piece.astype(jnp.bfloat16)


def whiten(dead_counts, partner, x):
    first, twiddle, second = forward_constants()
    count, width, _ = x.shape
    rounds = partner.shape[0]
    rows = R1 * (width + 8)
    vmem = pl.BlockSpec(memory_space=pltpu.VMEM)
    smem = pl.BlockSpec(memory_space=pltpu.SMEM)
    return pl.pallas_call(
        functools.partial(whiten_kernel, count),
        out_shape=(jax.ShapeDtypeStruct((HALF, width, 2 * R2), jnp.bfloat16),) * 2
        + (jax.ShapeDtypeStruct((1,), jnp.int32),) * rounds,
        in_specs=[smem] * 2 + [vmem] * 4,
        out_specs=(vmem, vmem) + (smem,) * rounds,
        scratch_shapes=[
            pltpu.VMEM((rows, SEG), jnp.float32),
            pltpu.VMEM((rows, 2 * R2), jnp.float32),
        ],
    )(
        dead_counts,
        partner,
        x,
        jnp.asarray(first, jnp.bfloat16),
        jnp.asarray(twiddle, jnp.float32),
        jnp.asarray(second, jnp.bfloat16),
    )


def quarter_turn(panel):
    lanes = panel.shape[1]
    wide = pltpu.roll(panel.astype(jnp.float32), lanes // 2, 1)
    left = lax.broadcasted_iota(jnp.int32, panel.shape, 1) < lanes // 2
    return jnp.where(left, wide, -wide).astype(jnp.bfloat16)


def correlate_kernel(partner_ref, low_ref, high_ref, *refs):
    rounds = len(refs) - 9
    their_refs = refs[:rounds]
    ta_ref, tb_hbm, lag_ref, o_ref, aa, bb, ss, tb_ref, tb_sem = refs[rounds:]
    fetch = pltpu.make_async_copy(tb_hbm, tb_ref, tb_sem)
    fetch.start()
    parts, _, width, lanes = low_ref.shape
    channels = parts * width
    pairs = rounds * width
    step = aa.shape[0] // (2 * R1)
    slots = [partner_ref[turn, 0] % 2 for turn in range(rounds)]

    def times(table, panel):
        return lax.dot_general(
            table, panel, (((1,), (1,)), ((), ())), preferred_element_type=jnp.float32
        )

    def own_pair(p, q):
        return low_ref[:, p].reshape(channels, lanes), high_ref[:, q].reshape(channels, lanes)

    def their_pair(p, q):
        return tuple(
            jnp.concatenate([ref[slot, half, k] for ref, slot in zip(their_refs, slots)], axis=0)
            for half, k in ((0, p), (1, q))
        )

    def product(table, first, second, signs):
        one, two = quarter_turn(first), quarter_turn(second)
        rows = {0: [first, second], 1: [one, -two], -1: [-one, two]}
        rows = [jnp.concatenate(rows[sign], axis=1) for sign in signs]
        return times(table, jnp.concatenate(rows, axis=0))

    def transforms(table_ref, pair, signs, keep):
        first, second = pair(0, 0)
        keep(
            0,
            product(table_ref[0], first, second, signs)
            + product(table_ref[HALF], second, first, signs),
        )

        def transform(p, carry):
            keep(p, product(table_ref[p], *pair(p, HALF - p), signs))
            return carry

        lax.fori_loop(1, HALF, transform, 0, unroll=5)

    odd = lax.broadcasted_iota(jnp.int32, (SEG, 4 * pairs), 1) // pairs % 2 == 1

    def keep_own(p, part):
        for h in range(2):
            for e in range(2):
                start = pl.multiple_of((2 * HALF * e + HALF * h + p) * step, 8)
                aa[pl.ds(start, SEG), :] = part[
                    h * SEG : (h + 1) * SEG, e * channels : (e + 1) * channels
                ]

    def keep_their(p, part):
        for h in range(2):
            start = pl.multiple_of((HALF * h + p) * step, 8)
            kept = part[h * SEG : (h + 1) * SEG]
            bb[pl.ds(start, SEG), :] = jnp.where(odd, -kept, kept) if h else kept

    transforms(ta_ref, own_pair, (0, 1), keep_own)
    fetch.wait()
    transforms(tb_ref, their_pair, (0, -1, 1, 0), keep_their)
    gap = ss.shape[0] // (2 * SEG)

    def multiply(f, carry):
        mine = aa[pl.ds(f, 2 * R1, stride=step), :].astype(jnp.bfloat16)
        their = bb[pl.ds(f, R1, stride=step), :]
        their = jnp.concatenate([their[:, : 2 * pairs], their[:, 2 * pairs :]], axis=0)
        product = lax.dot_general(
            their.astype(jnp.bfloat16),
            mine,
            (((0,), (0,)), ((), ())),
            preferred_element_type=jnp.float32,
        )
        for part in range(2):
            start = pl.multiple_of((2 * f + part) * gap, 8)
            ss[pl.ds(start, pairs), :] = product[part * pairs : (part + 1) * pairs]
        return carry

    lax.fori_loop(0, SEG, multiply, 0, unroll=8)

    for b in range(width):
        pieces = [
            ss[pl.ds(turn * width + b, 2 * SEG, stride=gap), :].astype(jnp.bfloat16)
            for turn in range(rounds)
        ]
        start = b * rounds * channels
        o_ref[:, start : start + rounds * channels] = jnp.dot(
            lag_ref[...], jnp.concatenate(pieces, axis=1), preferred_element_type=jnp.float32
        )


def correlate(partner, low, high, theirs):
    parts, _, width, lanes = low.shape
    channels = parts * width
    rounds = len(theirs)
    vmem = pl.BlockSpec(memory_space=pltpu.VMEM)
    return pl.pallas_call(
        correlate_kernel,
        out_shape=jax.ShapeDtypeStruct((LAGS, width * rounds * channels), jnp.float32),
        in_specs=[pl.BlockSpec(memory_space=pltpu.SMEM)]
        + [vmem] * (rounds + 3)
        + [pl.BlockSpec(memory_space=pl.ANY), vmem],
        out_specs=vmem,
        scratch_shapes=[
            pltpu.VMEM((2 * R1 * (SEG + 8), channels), jnp.float32),
            pltpu.VMEM((R1 * (SEG + 8), 4 * rounds * width), jnp.float32),
            pltpu.VMEM((2 * SEG * (rounds * width + 8), channels), jnp.float32),
            pltpu.VMEM((HALF + 1, 2 * SEG, 4 * R2), jnp.bfloat16),
            pltpu.SemaphoreType.DMA,
        ],
        compiler_params=pltpu.CompilerParams(vmem_limit_bytes=58 * 2**20),
    )(
        partner,
        low,
        high,
        *theirs,
        jnp.asarray(segment_table(-LAGS // 2, SEG + LAGS // 2), jnp.bfloat16),
        jnp.asarray(segment_table(0, SEG), jnp.bfloat16),
        jnp.asarray(lag_table(), jnp.bfloat16),
    )


def per_device(strain, dead_counts, partner):
    channels = strain.shape[0]
    count, blocks = lax.axis_size("tm"), lax.axis_size("chan")
    width = channels // count
    low, high, *indices = whiten(dead_counts, partner, scatter(strain, count, width))
    routes = [functools.partial(swap, bits, count) for bits in range(0, blocks, 2)]
    theirs, own = [], []
    for mine, index in zip((low, high), indices):
        their, part = lax.switch(index[0], routes, low, high, mine)
        theirs.append(their)
        own.append(part)
    return correlate(partner, *own, theirs)


def solution(mesh):
    return jax.shard_map(
        per_device,
        mesh=mesh,
        in_specs=(P("chan", "tm"), P("chan"), P()),
        out_specs=P(None, ("chan", "tm")),
        check_vma=False,
    )
```

```python
import functools
import math

import jax
import jax.numpy as jnp
import numpy as np
from jax import lax
from jax.experimental import pallas as pl
from jax.experimental.pallas import tpu as pltpu
from jax.sharding import PartitionSpec as P

NF = 2048
WH = 32
LAGS = 128
NT = 4096
epsilon = 1e-05

R1 = 32
R2 = NF // R1
SEG = NT // R1
HALF = R1 // 2


def split_bf16(table):
    table = np.asarray(table, np.float32)
    high = table.astype(np.dtype(jnp.bfloat16)).astype(np.float32)
    return high, table - high


@functools.cache
def forward_constants():
    kappa, t1 = np.arange(R1), np.arange(R1)
    phase = 2 * np.pi * (kappa[:, None] * t1[None, :] % R1) / R1
    first = np.concatenate([np.cos(phase), -np.sin(phase)], axis=0)
    first = np.concatenate(split_bf16(first), axis=0)
    t0 = np.arange(SEG)
    phase = 2 * np.pi * (kappa[:, None] * t0[None, :]) / NT
    amplitude = 1 / math.sqrt(NT)
    twiddle = np.stack([np.cos(phase) * amplitude, np.sin(phase) * amplitude])
    k2 = np.arange(R2)
    phase = 2 * np.pi * (t0[:, None] * k2[None, :] % SEG) / SEG
    cos, sin = np.cos(phase), np.sin(phase)
    second = np.block([[cos, -sin], [sin, cos]])
    second = np.concatenate(split_bf16(second), axis=1)
    return first.astype(np.float32), twiddle.astype(np.float32), second.astype(np.float32)


def window_sums(low, high):
    x = np.arange(-2 * NT, 2 * NT)
    u = np.arange(low, high)
    return np.exp(2j * np.pi * (x[:, None] * u[None, :] % NT) / NT).sum(1)


@functools.cache
def segment_table(low, high):
    sums = window_sums(low, high)
    f, k2 = np.arange(SEG), np.arange(R2)
    out = np.zeros((HALF + 1, 2, SEG, 2, 2, R2))
    for p in range(HALF + 1):
        classes = (p % HALF, R1 - p if p % HALF else HALF)
        for h, target in enumerate(classes):
            for g in range(2):
                if p % HALF:
                    source, mirrored = classes[g], g != h
                elif g == h and p == 0:
                    source, mirrored = target, False
                elif g != h and p == HALF:
                    source, mirrored = target, True
                else:
                    continue
                k = (-1 if mirrored else 1) * (source + R1 * k2)
                part = sums[k[None, :] - R1 // 2 * f[:, None] - R1 // 4 + 2 * NT]
                if source == 0:
                    part[:, 0] *= 0.0 if mirrored else math.sqrt(2.0)
                out[p, h, :, g, 0] = part.real
                out[p, h, :, g, 1] = part.imag if mirrored else -part.imag
    return out.reshape(HALF + 1, 2 * SEG, 4 * R2).astype(np.float32)


@functools.cache
def lag_table():
    tau, f = np.arange(LAGS) - LAGS // 2, np.arange(SEG)
    phase = 2 * np.pi * (f[None, :] + 0.5) * tau[:, None] / (2 * SEG)
    table = np.stack([np.cos(phase), -np.sin(phase)], axis=-1)
    scale = 1 / (2.0**19 * math.sqrt(2.0))
    return (table * scale).reshape(LAGS, 2 * SEG).astype(np.float32)


MESH = pl.DeviceIdType.MESH


def signal(**target):
    barrier = pltpu.get_barrier_semaphore()
    pl.semaphore_signal(barrier, inc=1, device_id=target, device_id_type=MESH)


def send(src, dst, sems, index, **target):
    copy = pltpu.make_async_remote_copy(
        src_ref=src,
        dst_ref=dst,
        send_sem=sems[0].at[index],
        recv_sem=sems[1].at[index],
        device_id=target,
        device_id_type=MESH,
    )
    copy.start()
    return copy


def scatter_kernel(count, width, x_ref, o_ref, send_sem, recv_sem, own_sem):
    me = lax.axis_index("tm")
    peers = [lax.rem(me + step, count) for step in range(1, count)]
    for peer in peers:
        signal(tm=peer)
    pl.semaphore_wait(pltpu.get_barrier_semaphore(), len(peers))

    def rows(index):
        return x_ref.at[pl.ds(pl.multiple_of(index * width, width), width), :]

    copies = [
        send(rows(peer), o_ref.at[me], (send_sem, recv_sem), step, tm=peer)
        for step, peer in enumerate(peers)
    ]
    own = pltpu.make_async_copy(rows(me), o_ref.at[me], own_sem)
    own.start()
    own.wait()
    for copy in copies:
        copy.wait()


def scatter(strain, count, width):
    return pl.pallas_call(
        functools.partial(scatter_kernel, count, width),
        out_shape=jax.ShapeDtypeStruct((count, width, strain.shape[1]), strain.dtype),
        in_specs=[pl.BlockSpec(memory_space=pl.ANY)],
        out_specs=pl.BlockSpec(memory_space=pl.ANY),
        scratch_shapes=[
            pltpu.SemaphoreType.DMA((count,)),
            pltpu.SemaphoreType.DMA((count,)),
            pltpu.SemaphoreType.DMA,
        ],
        compiler_params=pltpu.CompilerParams(
            collective_id=32, has_side_effects=True, skip_device_barrier=True
        ),
    )(strain)


def swap_kernel(bits, count, low_ref, high_ref, mine_ref, their_ref, all_ref, *sems):
    pair_sems, over_sems, ring_sems, own_sem = sems[0:2], sems[2:4], sems[4:6], sems[6]
    me, block = lax.axis_index("tm"), lax.axis_index("chan")
    right, left = lax.rem(me + 2, count), lax.rem(me + count - 2, count)
    side = me + 1 - 2 * (me % 2)
    partner = block
    for digit in range(bits.bit_length()):
        if bits >> digit & 1:
            partner = partner + 2**digit * (1 - 2 * (block // 2**digit % 2))
    beside = block + 1 - 2 * (block % 2)
    for peer in (right, left, side):
        signal(tm=peer)
    signal(chan=beside)
    if bits:
        signal(chan=partner)
    pl.semaphore_wait(pltpu.get_barrier_semaphore(), 4 + (bits > 0))
    size = mine_ref.shape[0] // 2
    chunks = [pl.ds(chunk * size, size) for chunk in range(2)]
    left_side, right_side = (peer + 1 - 2 * (peer % 2) for peer in (left, right))

    def give(index, owner, chunk, peer, src=None):
        dst = all_ref.at[owner, chunks[chunk]]
        return send(dst if src is None else src.at[chunks[chunk]], dst, ring_sems, index, tm=peer)

    to_side, to_right, to_left = [], [], []
    for chunk in range(2):
        to_side.append(give(chunk, me, chunk, side, mine_ref))
        to_right.append(give(2 + chunk, me, chunk, right, mine_ref))
        to_left.append(give(4 + chunk, me, chunk, left, mine_ref))
    halves = (low_ref, high_ref)
    if bits:
        pair = [
            send(half, their_ref.at[0, h], pair_sems, h, chan=partner)
            for h, half in enumerate(halves)
        ]
    else:
        pair = [
            pltpu.make_async_copy(half, their_ref.at[0, h], pair_sems[0].at[h])
            for h, half in enumerate(halves)
        ]
        for copy in pair:
            copy.start()
    own = pltpu.make_async_copy(mine_ref, all_ref.at[me], own_sem)
    own.start()
    onward, far = [], []
    for chunk in range(2):
        to_side[chunk].wait_recv()
        onward.append(give(6 + chunk, side, chunk, right))
        onward.append(give(8 + chunk, side, chunk, left))
        if chunk == 0:
            to_right[0].wait_recv()
            far.append(give(10, left, 0, right))
        else:
            to_left[1].wait_recv()
            far.append(give(11, right, 1, left))
    onward[0].wait_recv()
    far.append(give(12, left_side, 0, right))
    onward[3].wait_recv()
    far.append(give(13, right_side, 1, left))
    over = []
    for h, copy in enumerate(pair):
        if bits:
            copy.wait_recv()
        else:
            copy.wait()
        over.append(send(their_ref.at[0, h], their_ref.at[1, h], over_sems, h, chan=beside))
    for copy in (to_right[1], to_left[0], onward[1], onward[2]):
        copy.wait_recv()
    for copy in to_side + to_right + to_left + onward:
        copy.wait_send()
    if bits:
        for copy in pair:
            copy.wait_send()
    own.wait()
    for copy in far + over:
        copy.wait()


def swap(bits, count, low, high, mine):
    here = pl.BlockSpec(memory_space=pltpu.VMEM)
    there = pl.BlockSpec(memory_space=pl.ANY)
    return pl.pallas_call(
        functools.partial(swap_kernel, bits, count),
        out_shape=(
            jax.ShapeDtypeStruct((2, 2) + low.shape, low.dtype),
            jax.ShapeDtypeStruct((count,) + low.shape, low.dtype),
        ),
        in_specs=[here] * 3,
        out_specs=(there, there),
        scratch_shapes=[
            pltpu.SemaphoreType.DMA((2,)),
            pltpu.SemaphoreType.DMA((2,)),
            pltpu.SemaphoreType.DMA((2,)),
            pltpu.SemaphoreType.DMA((2,)),
            pltpu.SemaphoreType.DMA((14,)),
            pltpu.SemaphoreType.DMA((14,)),
            pltpu.SemaphoreType.DMA,
        ],
        compiler_params=pltpu.CompilerParams(
            collective_id=bits // 2, has_side_effects=True, skip_device_barrier=True
        ),
    )(low, high, mine)


def whiten_kernel(
    count, dead_ref, partner_ref, x_ref, first_ref, twiddle_ref, second_ref, *refs
):
    low_ref, high_ref, *index_refs, flat, spec = refs
    for turn, index_ref in enumerate(index_refs):
        index_ref[0] = partner_ref[turn, 0] // 2
    blocks, width, samples = x_ref.shape
    step = flat.shape[0] // R1
    per = samples // SEG
    limit = count * width - dead_ref[0] - lax.axis_index("tm") * width
    for j in range(blocks):
        for q in range(per):
            start = (j * per + q) * step
            flat[start : start + width, :] = x_ref[j, :, q * SEG : (q + 1) * SEG].astype(
                jnp.float32
            )
    cos, sin = twiddle_ref[0], twiddle_ref[1]
    turned = []
    for c in range(width):
        series = flat[pl.ds(c, R1, stride=step), :].astype(jnp.bfloat16)
        part = jnp.dot(first_ref[...], series, preferred_element_type=jnp.float32)
        real = part[:R1] + part[2 * R1 : 3 * R1]
        imag = part[R1 : 2 * R1] + part[3 * R1 :]
        turned.append(
            jnp.concatenate([real * cos + imag * sin, imag * cos - real * sin], axis=1)
        )
    turned = jnp.concatenate(turned, axis=0)
    high = turned.astype(jnp.bfloat16)
    low = (turned - high.astype(jnp.float32)).astype(jnp.bfloat16)
    both = jnp.dot(high, second_ref[...], preferred_element_type=jnp.float32)
    result = jnp.dot(low, second_ref[:, : 2 * R2], preferred_element_type=jnp.float32)
    result = result + both[:, 2 * R2 :] + both[:, : 2 * R2]
    for c in range(width):
        spec[pl.ds(c, R1, stride=step), :] = result[c * R1 : (c + 1) * R1]
    lane = lax.broadcasted_iota(jnp.int32, (width, 2 * R2), 1) % R2
    channel = lax.broadcasted_iota(jnp.int32, (width, 2 * R2), 0)
    alive = (channel < limit).astype(jnp.float32)
    power = []
    for kappa in range(R1):
        square = jnp.square(spec[kappa * step : kappa * step + width, :])
        power.append(square + pltpu.roll(square, R2, 1))
    upto, total = [], None
    for kappa in range(R1):
        total = power[kappa] if total is None else total + power[kappa]
        upto.append(total)
    rest = None
    for kappa in reversed(range(R1)):
        rest = power[kappa] if rest is None else rest + power[kappa]
        below = jnp.where(lane == 0, 0.0, pltpu.roll(rest, 1, 1))
        above = jnp.where(lane == R2 - 1, 0.0, pltpu.roll(upto[kappa], 2 * R2 - 1, 1))
        smooth = (below + total + above) * (1.0 / (2 * WH + 1))
        factor = alive * lax.rsqrt(smooth + epsilon)
        piece = spec[kappa * step : kappa * step + width, :] * factor
        half_ref = (low_ref, high_ref)[kappa // HALF]
        half_ref[kappa % HALF] = piece.astype(jnp.bfloat16)


def whiten(dead_counts, partner, x):
    first, twiddle, second = forward_constants()
    count, width, _ = x.shape
    rounds = partner.shape[0]
    rows = R1 * (width + 8)
    vmem = pl.BlockSpec(memory_space=pltpu.VMEM)
    smem = pl.BlockSpec(memory_space=pltpu.SMEM)
    return pl.pallas_call(
        functools.partial(whiten_kernel, count),
        out_shape=(jax.ShapeDtypeStruct((HALF, width, 2 * R2), jnp.bfloat16),) * 2
        + (jax.ShapeDtypeStruct((1,), jnp.int32),) * rounds,
        in_specs=[smem] * 2 + [vmem] * 4,
        out_specs=(vmem, vmem) + (smem,) * rounds,
        scratch_shapes=[
            pltpu.VMEM((rows, SEG), jnp.float32),
            pltpu.VMEM((rows, 2 * R2), jnp.float32),
        ],
    )(
        dead_counts,
        partner,
        x,
        jnp.asarray(first, jnp.bfloat16),
        jnp.asarray(twiddle, jnp.float32),
        jnp.asarray(second, jnp.bfloat16),
    )


def quarter_turn(panel):
    lanes = panel.shape[1]
    wide = pltpu.roll(panel.astype(jnp.float32), lanes // 2, 1)
    left = lax.broadcasted_iota(jnp.int32, panel.shape, 1) < lanes // 2
    return jnp.where(left, wide, -wide).astype(jnp.bfloat16)


def correlate_kernel(partner_ref, low_ref, high_ref, *refs):
    rounds = len(refs) - 10
    their_refs = refs[:rounds]
    ta_hbm, tb_hbm, lag_ref, o_ref, aa, bb, ss, ta_ref, tb_ref, table_sem = refs[rounds:]
    fetches = []
    for part, (start, size) in enumerate(((0, 1), (HALF, 1), (1, 5), (6, HALF - 6))):
        for side, (table, kept) in enumerate(((ta_hbm, ta_ref), (tb_hbm, tb_ref))):
            rows = pl.ds(start, size)
            fetches.append(
                pltpu.make_async_copy(table.at[rows], kept.at[rows], table_sem.at[side, part])
            )
            fetches[-1].start()
    parts, _, width, lanes = low_ref.shape
    channels = parts * width
    pairs = rounds * width
    step = aa.shape[0] // (2 * R1)
    slots = [partner_ref[turn, 0] % 2 for turn in range(rounds)]

    def times(table, panel):
        return lax.dot_general(
            table, panel, (((1,), (1,)), ((), ())), preferred_element_type=jnp.float32
        )

    def own_pair(p, q):
        return low_ref[:, p].reshape(channels, lanes), high_ref[:, q].reshape(channels, lanes)

    def their_pair(p, q):
        return tuple(
            jnp.concatenate([ref[slot, half, k] for ref, slot in zip(their_refs, slots)], axis=0)
            for half, k in ((0, p), (1, q))
        )

    def product(table, first, second, signs):
        one, two = quarter_turn(first), quarter_turn(second)
        rows = {0: [first, second], 1: [one, -two], -1: [-one, two]}
        rows = [jnp.concatenate(rows[sign], axis=1) for sign in signs]
        return times(table, jnp.concatenate(rows, axis=0))

    odd = lax.broadcasted_iota(jnp.int32, (SEG, 4 * pairs), 1) // pairs % 2 == 1

    def keep_own(p, part):
        for h in range(2):
            for e in range(2):
                start = pl.multiple_of((2 * HALF * e + HALF * h + p) * step, 8)
                aa[pl.ds(start, SEG), :] = part[
                    h * SEG : (h + 1) * SEG, e * channels : (e + 1) * channels
                ]

    def keep_their(p, part):
        for h in range(2):
            start = pl.multiple_of((HALF * h + p) * step, 8)
            kept = part[h * SEG : (h + 1) * SEG]
            bb[pl.ds(start, SEG), :] = jnp.where(odd, -kept, kept) if h else kept

    sides = (
        (ta_ref, own_pair, (0, 1), keep_own),
        (tb_ref, their_pair, (0, -1, 1, 0), keep_their),
    )
    for fetch in fetches[:4]:
        fetch.wait()
    for table_ref, pair, signs, keep in sides:
        first, second = pair(0, 0)
        bins = product(table_ref[0], first, second, signs)
        keep(0, bins + product(table_ref[HALF], second, first, signs))

    def transform(p, carry=0):
        for table_ref, pair, signs, keep in sides:
            keep(p, product(table_ref[p], *pair(p, HALF - p), signs))
        return carry

    for fetch in fetches[4:6]:
        fetch.wait()
    for p in range(1, 6):
        transform(p)
    for fetch in fetches[6:]:
        fetch.wait()
    lax.fori_loop(6, HALF, transform, 0, unroll=5)
    gap = ss.shape[0] // (2 * SEG)

    def multiply(f, carry):
        mine = aa[pl.ds(f, 2 * R1, stride=step), :].astype(jnp.bfloat16)
        their = bb[pl.ds(f, R1, stride=step), :]
        their = jnp.concatenate([their[:, : 2 * pairs], their[:, 2 * pairs :]], axis=0)
        product = lax.dot_general(
            their.astype(jnp.bfloat16),
            mine,
            (((0,), (0,)), ((), ())),
            preferred_element_type=jnp.float32,
        )
        for part in range(2):
            start = pl.multiple_of((2 * f + part) * gap, 8)
            ss[pl.ds(start, pairs), :] = product[part * pairs : (part + 1) * pairs]
        return carry

    lax.fori_loop(0, SEG, multiply, 0, unroll=8)

    for b in range(width):
        pieces = [
            ss[pl.ds(turn * width + b, 2 * SEG, stride=gap), :].astype(jnp.bfloat16)
            for turn in range(rounds)
        ]
        start = b * rounds * channels
        o_ref[:, start : start + rounds * channels] = jnp.dot(
            lag_ref[...], jnp.concatenate(pieces, axis=1), preferred_element_type=jnp.float32
        )


def correlate(partner, low, high, theirs):
    parts, _, width, lanes = low.shape
    channels = parts * width
    rounds = len(theirs)
    vmem = pl.BlockSpec(memory_space=pltpu.VMEM)
    return pl.pallas_call(
        correlate_kernel,
        out_shape=jax.ShapeDtypeStruct((LAGS, width * rounds * channels), jnp.float32),
        in_specs=[pl.BlockSpec(memory_space=pltpu.SMEM)]
        + [vmem] * (rounds + 2)
        + [pl.BlockSpec(memory_space=pl.ANY)] * 2
        + [vmem],
        out_specs=vmem,
        scratch_shapes=[
            pltpu.VMEM((2 * R1 * (SEG + 8), channels), jnp.float32),
            pltpu.VMEM((R1 * (SEG + 8), 4 * rounds * width), jnp.float32),
            pltpu.VMEM((2 * SEG * (rounds * width + 8), channels), jnp.float32),
            pltpu.VMEM((HALF + 1, 2 * SEG, 4 * R2), jnp.bfloat16),
            pltpu.VMEM((HALF + 1, 2 * SEG, 4 * R2), jnp.bfloat16),
            pltpu.SemaphoreType.DMA((2, 4)),
        ],
        compiler_params=pltpu.CompilerParams(vmem_limit_bytes=58 * 2**20),
    )(
        partner,
        low,
        high,
        *theirs,
        jnp.asarray(segment_table(-LAGS // 2, SEG + LAGS // 2), jnp.bfloat16),
        jnp.asarray(segment_table(0, SEG), jnp.bfloat16),
        jnp.asarray(lag_table(), jnp.bfloat16),
    )


def per_device(strain, dead_counts, partner):
    channels = strain.shape[0]
    count, blocks = lax.axis_size("tm"), lax.axis_size("chan")
    width = channels // count
    low, high, *indices = whiten(dead_counts, partner, scatter(strain, count, width))
    routes = [functools.partial(swap, bits, count) for bits in range(0, blocks, 2)]
    theirs, own = [], []
    for mine, index in zip((low, high), indices):
        their, part = lax.switch(index[0], routes, low, high, mine)
        theirs.append(their)
        own.append(part)
    return correlate(partner, *own, theirs)


def solution(mesh):
    return jax.shard_map(
        per_device,
        mesh=mesh,
        in_specs=(P("chan", "tm"), P("chan"), P()),
        out_specs=P(None, ("chan", "tm")),
        check_vma=False,
    )
```
